32 devices in a mesh: row: 2 (over y), col: 8 (over z, x), leaf: 2 (over core).
Axes of the slice: x: 2, y: 2, z: 4, core: 2. Of those that a mesh axis runs over, the one named last changes fastest.
Arguments:
- leaf_rhs: float32 [2, 2, 2, 256, 512], P('leaf', None, None, 'col'), may hold values from -6 to 6
- root_rhs: float32 [2, 2, 256, 512], P(None, None, 'col'), may hold values from -6 to 6
- leaf_inverses: float32 [2, 2, 2, 256, 512], P('leaf', None, None, 'col', 'row'), may hold values from -0.02 to 2, as said below
- root_inverses: float32 [2, 2, 256, 512], P(None, None, 'col', 'row'), may hold values from -0.02 to 2, as said below
- leaf_blocks: float32 [2, 5, 2, 256, 512], P('leaf', None, None, 'col', 'row'), may hold values from -0.375 to 0.375
- root_block: float32 [2, 256, 512], P(None, 'col', 'row'), may hold values from -0.25 to 0.25
- pattern: int32 [2, 5, 4, 8], P('leaf', None, 'row', 'col'), may hold values 0 or 1
Outputs:
- leaf_solution: float32 [2, 2, 2, 256, 512], P('leaf', None, None, 'col')
- root_solution: float32 [2, 2, 256, 512], P(None, None, 'col')
The draws below stay inside these ranges and needn't reach their ends.
Inputs may be any that keep to these rules, and one draw needn't show every extreme that they name: `leaf_inverses`: lower triangular as a 512 x 512 matrix, diagonal entries between 1 and 2. `root_inverses`: lower triangular as a 512 x 512 matrix, diagonal entries between 1 and 2.
All inputs are finite; a program needn't handle non-finite values. No bound on the sum of `pattern` on one device may be relied on, other than what follows from the above.
Results may differ from the reference program's by a relative error of at most 0.00017.
Values sent between devices are 32-bit elements; how exact they have to be, the bound alone decides.
No kernel may reach another device: no remote copies, remote signals or barrier semaphores. Data moves between devices by JAX's collectives and lax.ppermute only.
A program may use at most 64 MiB of HBM per device.

```python
import jax
import jax.numpy as jnp
from jax import lax

BLK = 128
NRHS = 512
QR = 32
GRID_ROWS = 2
NLEAF = 2
SEG = 256
SW = 512
N_COL = 8


def index_rows(order):
    return jnp.broadcast_to(jnp.arange(order)[:, None], (order, order))


def lower_inverses(key, count):
    first, second = jax.random.split(key)
    lower = jax.random.uniform(first, (count, SW, SW), jnp.float32, -0.02, 0.02)
    diagonal = jax.random.uniform(second, (count, SW, SW), jnp.float32, 1.0, 2.0)
    rows = index_rows(SW)
    cols = rows.T
    built = jnp.where(rows > cols, lower, 0.0) + jnp.where(rows == cols, diagonal, 0.0)
    stored = jnp.swapaxes(built, 1, 2)
    return stored.reshape(count, GRID_ROWS, SEG, SW)


def draw_leaf_inverses(key, part):
    return lower_inverses(jax.random.fold_in(key, 11), NLEAF * 2).reshape(NLEAF, 2, GRID_ROWS, SEG, SW)


def draw_root_inverses(key, part):
    return lower_inverses(jax.random.fold_in(key, 23), 2)


def set_ends(entries, own_key, low, largest):
    extent = entries.shape
    index_at = [jax.random.randint(jax.random.fold_in(own_key, axis), (), 0, extent[axis]) for axis in range(len(extent))]
    entries = entries.at[tuple(index_at)].set(low)
    longest = extent.index(max(extent))
    index_at[longest] = (index_at[longest] + 1) % extent[longest]
    return entries.at[tuple(index_at)].set(largest)


def steps_of(own_key, extent, shards, low, largest):
    def one(position, blocks):
        heights = jax.random.uniform(jax.random.fold_in(jax.random.fold_in(own_key, 6), position), (blocks,), jnp.float32, low / len(shards), largest / len(shards))
        return jnp.repeat(jnp.exp(heights), extent[position] // blocks).reshape((-1,) + (1,) * (len(extent) - position - 1))

    level = one(*shards[0])
    for cut in shards[1:]:
        level = level * one(*cut)
    return level


def centred(key, dims, deviation, most, pieces=(), held_as=jnp.bfloat16):
    array = jax.random.normal(key, dims, jnp.float32) * deviation
    if len(pieces) > 0:
        array = steps_of(key, dims, pieces, -0.22, 0.18) * array
    return jnp.clip(array, min=-most, max=most).astype(held_as)


def setup_inputs(seed: int = 0) -> dict:
    splits = jax.random.split(jax.random.key(seed), 8)
    leaf_rhs = centred(splits[0], (NLEAF, 2, GRID_ROWS, SEG, NRHS), 1.0, 6.0, ((0, 2), (3, 8)), jnp.float32)
    root_rhs = centred(splits[1], (2, GRID_ROWS, SEG, NRHS), 1.0, 6.0, ((2, 8),), jnp.float32)
    leaf_inverses = draw_leaf_inverses(jax.random.fold_in(splits[7], 71), 0)
    root_inverses = draw_root_inverses(jax.random.fold_in(splits[7], 71), 0)
    leaf_blocks = centred(splits[4], (NLEAF, 5, GRID_ROWS, SEG, SW), (SW // 2) ** -0.5, 0.375, ((0, 2), (3, 8), (4, 2)), jnp.float32)
    root_block = centred(splits[5], (GRID_ROWS, SEG, SW), SW ** -0.5, 0.25, ((1, 8), (2, 2)), jnp.float32)
    pattern = set_ends((jax.random.randint(splits[6], (NLEAF, 5, SW // BLK, N_COL), 0, 2) < 1).astype(jnp.int32), jax.random.fold_in(splits[6], 1), 0, 1)
    return dict(leaf_rhs=leaf_rhs, root_rhs=root_rhs, leaf_inverses=leaf_inverses, root_inverses=root_inverses, leaf_blocks=leaf_blocks, root_block=root_block, pattern=pattern)


def product(block, vector):
    matrix = block.reshape(SW, SW).T
    whole = jnp.dot(matrix, vector.reshape(SW, NRHS), precision=lax.Precision.HIGHEST, preferred_element_type=jnp.float32)
    return whole.reshape(GRID_ROWS, SEG, NRHS)


def masked_block(block, tiles):
    shaped = block.reshape(GRID_ROWS, N_COL, QR, SW // BLK, BLK)
    weights = tiles.astype(jnp.float32).T[None, :, None, :, None]
    return (shaped * weights).reshape(GRID_ROWS, SEG, SW)


def reference(leaf_rhs, root_rhs, leaf_inverses, root_inverses, leaf_blocks, root_block, pattern):
    leaf_out = []
    upper_two = jnp.zeros((GRID_ROWS, SEG, NRHS), jnp.float32)
    upper_three = jnp.zeros((GRID_ROWS, SEG, NRHS), jnp.float32)
    for subtree in range(NLEAF):
        blocks = [masked_block(leaf_blocks[subtree, m], pattern[subtree, m]) for m in range(5)]
        first = product(leaf_inverses[subtree, 0], leaf_rhs[subtree, 0])
        second = product(leaf_inverses[subtree, 1], leaf_rhs[subtree, 1] - product(blocks[0], first))
        upper_two = upper_two + product(blocks[1], first) + product(blocks[2], second)
        upper_three = upper_three + product(blocks[3], first) + product(blocks[4], second)
        leaf_out.append(jnp.stack([first, second]))
    third = product(root_inverses[0], root_rhs[0] - upper_two)
    fourth = product(root_inverses[1], root_rhs[1] - upper_three - product(root_block, third))
    return jnp.stack(leaf_out), jnp.stack([third, fourth])
```

```python
import functools

import jax
import jax.numpy as jnp
from jax import lax
from jax.experimental import pallas as pl
from jax.experimental.pallas import tpu as pltpu
from jax.sharding import PartitionSpec as P

BLK = 128
AXES = ("row", "col", "leaf")
F32 = jnp.float32
BF16 = jnp.bfloat16


def apply_rows(block, vector):
    block = block.reshape(-1, block.shape[-1])
    vector = vector.reshape(-1, vector.shape[-1])
    term = lax.dot_general(
        block,
        vector,
        (((0,), (0,)), ((), ())),
        precision=lax.Precision.HIGHEST,
        preferred_element_type=F32,
    )
    owned = lax.psum_scatter(term, "col", scatter_dimension=0, tiled=True)
    return lax.all_gather(owned[None], "row", axis=0, tiled=True)


def masked(leaf_blocks, pattern):
    local = leaf_blocks[0]
    shaped = local.reshape(local.shape[:3] + (local.shape[3] // BLK, BLK))
    weights = pattern[0].astype(F32).transpose(0, 2, 1)[:, None, :, :, None]
    return (shaped * weights).reshape(local.shape)


def general(leaf_rhs, root_rhs, leaf_inverses, root_inverses, leaf_blocks, root_block, pattern):
    blocks = masked(leaf_blocks, pattern)
    first = apply_rows(leaf_inverses[0, 0], leaf_rhs[0, 0])
    second = apply_rows(leaf_inverses[0, 1], leaf_rhs[0, 1] - apply_rows(blocks[0], first))
    upper_two = apply_rows(blocks[1], first) + apply_rows(blocks[2], second)
    upper_three = apply_rows(blocks[3], first) + apply_rows(blocks[4], second)
    upper_two, upper_three = lax.psum((upper_two, upper_three), "leaf")
    third = apply_rows(root_inverses[0], root_rhs[0] - upper_two)
    fourth = apply_rows(root_inverses[1], root_rhs[1] - upper_three - apply_rows(root_block, third))
    return (jnp.stack([first, second])[None], jnp.stack([third, fourth]))


def pairs(dest):
    out = []
    for r in range(2):
        for zh in range(2):
            for zl in range(2):
                for x in range(2):
                    for l in range(2):
                        d = dest(r, zh, zl, x, l)
                        if d is None:
                            continue
                        s = (r * 8 + zh * 4 + zl * 2 + x) * 2 + l
                        e = (d[0] * 8 + d[1] * 4 + d[2] * 2 + d[3]) * 2 + d[4]
                        out.append((s, e))
    return out


def send(value, dest):
    return lax.ppermute(value, AXES, pairs(dest))


def to_far(r, zh, zl, x, l):
    return r, zh ^ 1, zl, x, l


def to_second(r, zh, zl, x, l):
    return (r, zh, zl, x ^ 1, l) if l == 0 else (r ^ 1, zh, zl, x, l)


def to_third(r, zh, zl, x, l):
    return (r ^ 1, zh, zl, x, l) if l == 0 else (r, zh, zl, x ^ 1, l)


def to_pair(r, zh, zl, x, l):
    return r, zh, zl ^ 1, x, l


def to_core(r, zh, zl, x, l):
    return r, zh, zl, x, l ^ 1


def to_row(r, zh, zl, x, l):
    return r ^ 1, zh, zl, x, l


def to_group(b1, b2):
    return lambda r, zh, zl, x, l: (r, zh ^ b1, zl, x ^ b2, l)


def to_group_by_core(b1, b2):
    return lambda r, zh, zl, x, l: (r ^ l, zh ^ b1, zl, x ^ b2, l)


def gather_begin(local):
    return send(local, to_far)


def gather_rest(local, far):
    two = jnp.stack([local, far])
    four = jnp.concatenate([two, send(two, to_second)])
    return four, send(four, to_third)


def vmem():
    return pl.BlockSpec(memory_space=pltpu.VMEM)


def anywhere():
    return pl.BlockSpec(memory_space=pl.ANY)


def smem():
    return pl.BlockSpec(memory_space=pltpu.SMEM)


def lanes_low():
    return lax.broadcasted_iota(jnp.int32, (1, 128), 1) < 64


def split(value):
    high = value.astype(BF16)
    return high, (value - high.astype(F32)).astype(BF16)


def dot3(left, right):
    lh, ll = left
    rh, rl = right
    whole = jnp.dot(lh, rl, preferred_element_type=F32)
    whole += jnp.dot(ll, rh, preferred_element_type=F32)
    return whole + jnp.dot(lh, rh, preferred_element_type=F32)


def step_kernel(vec_fn, terms, nvec, nchunk, nextra, where_ref, *refs):
    vecs = refs[:nvec]
    chunks = refs[nvec : nvec + 2 * nchunk]
    outs = refs[nvec + 2 * nchunk : nvec + 2 * nchunk + 2 + nextra]
    held, sems = refs[nvec + 2 * nchunk + 2 + nextra :]
    r, zh, zl, x, l = (where_ref[k] for k in range(5))
    copies = []
    for t, (chunk, m, _) in enumerate(terms):
        row = []
        for b3 in range(2):
            for b2 in range(2):
                for b1 in range(2):
                    rr = r ^ jnp.where(l == 0, b3, b2)
                    xx = x ^ jnp.where(l == 0, b2, b3)
                    copy = pltpu.make_async_copy(
                        chunks[2 * chunk + b3].at[b2 * 2 + b1, m],
                        held.at[t, rr, :, zh ^ b1, xx],
                        sems.at[t, b3 * 4 + b2 * 2 + b1],
                    )
                    copy.start()
                    row.append(copy)
        copies.append(row)
    sources, extras = vec_fn([v[...] for v in vecs])
    for k, value in enumerate(extras):
        outs[2 + k][...] = value
    halves = [
        split(jnp.concatenate([s[:64], s[64:]], axis=1)) for s in sources
    ]
    sums = [None, None]
    for t, (_, _, which) in enumerate(terms):
        for copy in copies[t]:
            copy.wait()
        for a in range(2):
            matrix = split(held[t, a].reshape(256, 256))
            part = dot3(halves[which], matrix)
            sums[a] = part if sums[a] is None else sums[a] + part
    whole = jnp.concatenate(sums, axis=0)
    one, two = whole[:, :128], whole[:, 128:]
    low = lanes_low()
    even = jnp.where(low, one, pltpu.roll(two, 64, 1))
    odd = jnp.where(low, pltpu.roll(one, 64, 1), two)
    outs[0][...] = jnp.where(zl == 0, even, odd)
    outs[1][...] = jnp.where(zl == 0, odd, even)


def step(name, where, vec_fn, vecs, chunks, terms, nextra=0):
    flat = [array for pair in chunks for array in pair]
    kernel = functools.partial(step_kernel, vec_fn, terms, len(vecs), len(chunks), nextra)
    shape = jax.ShapeDtypeStruct((128, 128), F32)
    return pl.pallas_call(
        kernel,
        out_shape=[shape] * (2 + nextra),
        in_specs=[smem()] + [vmem()] * len(vecs) + [anywhere()] * len(flat),
        out_specs=[vmem()] * (2 + nextra),
        scratch_shapes=[
            pltpu.VMEM((len(terms), 2, 2, 2, 2, 32, 256), F32),
            pltpu.SemaphoreType.DMA((len(terms), 8)),
        ],
        name=name,
    )(where, *vecs, *flat)


def cut_kernel(where_ref, leaf_ref, root_ref, *refs):
    outs, held = refs[:4], refs[4]
    r, zh, x = where_ref[0], where_ref[1], where_ref[3]
    low = lanes_low()
    for p in range(4):
        source = leaf_ref if p < 2 else root_ref
        for z in range(2):
            start = pl.multiple_of((2 * r + z) * 128, 128)
            one = source[p % 2, 0, :, pl.ds(start, 128)]
            two = source[p % 2, 1, :, pl.ds(start, 128)]
            held[2 * z, p] = jnp.where(low, one, pltpu.roll(two, 64, 1))
            held[2 * z + 1, p] = jnp.where(low, pltpu.roll(one, 64, 1), two)
    for b1 in range(2):
        for b2 in range(2):
            outs[b1 * 2 + b2][...] = held[(zh ^ b1) * 2 + (x ^ b2)]


def cut(where, leaf_rhs, root_rhs):
    shape = jax.ShapeDtypeStruct((4, 32, 128), F32)
    return pl.pallas_call(
        cut_kernel,
        out_shape=[shape] * 4,
        in_specs=[smem(), vmem(), vmem()],
        out_specs=[vmem()] * 4,
        scratch_shapes=[pltpu.VMEM((4, 4, 32, 128), F32)],
        name="cut_columns",
    )(where, leaf_rhs, root_rhs)


def stand_kernel(where_ref, *refs):
    pieces, outs, held = refs[:4], refs[4:8], refs[8]
    zh, x = where_ref[1], where_ref[3]
    for b1 in range(2):
        for b2 in range(2):
            held[(zh ^ b1) * 2 + (x ^ b2)] = pieces[b1 * 2 + b2][...]
    for p in range(4):
        outs[p][...] = held[:, p].reshape(128, 128).T


def stand(where, pieces):
    shape = jax.ShapeDtypeStruct((128, 128), F32)
    return pl.pallas_call(
        stand_kernel,
        out_shape=[shape] * 4,
        in_specs=[smem()] + [vmem()] * 4,
        out_specs=[vmem()] * 4,
        scratch_shapes=[pltpu.VMEM((4, 4, 32, 128), F32)],
        name="stand_columns",
    )(where, *pieces)


def lay_kernel(where_ref, *refs):
    first, keep, got = refs[:3]
    outs, held = refs[3:7], refs[7]
    zh, x = where_ref[1], where_ref[3]
    for p, value in enumerate((first[...], keep[...] + got[...])):
        held[:, p] = value.T.reshape(4, 32, 128)
    for b1 in range(2):
        for b2 in range(2):
            outs[b1 * 2 + b2][...] = held[(zh ^ b1) * 2 + (x ^ b2)]


def lay(name, where, first, keep, got):
    shape = jax.ShapeDtypeStruct((2, 32, 128), F32)
    return pl.pallas_call(
        lay_kernel,
        out_shape=[shape] * 4,
        in_specs=[smem()] + [vmem()] * 3,
        out_specs=[vmem()] * 4,
        scratch_shapes=[pltpu.VMEM((4, 2, 32, 128), F32)],
        name=name,
    )(where, first, keep, got)


def join_kernel(where_ref, near_ref, other_ref, out_ref, held):
    r, zh, x = where_ref[0], where_ref[1], where_ref[3]
    for b1 in range(2):
        for b2 in range(2):
            place = (zh ^ b1) * 2 + (x ^ b2)
            held[r * 4 + place] = near_ref[b1 * 2 + b2]
            held[(r ^ 1) * 4 + place] = other_ref[b1 * 2 + b2]
    low = lanes_low()
    for p in range(2):
        for u in range(4):
            one, two = held[2 * u, p], held[2 * u + 1, p]
            out_ref[p, 0, :, u * 128 : u * 128 + 128] = jnp.where(low, one, pltpu.roll(two, 64, 1))
            out_ref[p, 1, :, u * 128 : u * 128 + 128] = jnp.where(low, pltpu.roll(one, 64, 1), two)


def join(name, where, near, other):
    return pl.pallas_call(
        join_kernel,
        out_shape=jax.ShapeDtypeStruct((2, 2, 32, 512), F32),
        in_specs=[smem()] + [vmem()] * 2,
        out_specs=vmem(),
        scratch_shapes=[pltpu.VMEM((8, 2, 32, 128), F32)],
        name=name,
    )(where, near, other)


def total(keep, got):
    return keep + got


def grouped(leaf_rhs, root_rhs, leaf_inverses, root_inverses, leaf_blocks, root_block, pattern):
    row, col, core = (lax.axis_index(name) for name in AXES)
    where = jnp.stack([row, col // 4, (col // 2) % 2, col % 2, core]).astype(jnp.int32)
    blocks = masked(leaf_blocks, pattern)
    inverses = leaf_inverses[0]
    chunk_a = jnp.stack([inverses[0], blocks[0]])
    chunk_b = jnp.stack([inverses[1], blocks[1], blocks[2]])
    chunk_c = jnp.concatenate([blocks[3:5], root_inverses, root_block[None]])

    far_a = gather_begin(chunk_a)
    mine = cut(where, leaf_rhs[0], root_rhs)
    pieces = [mine[0]] + [send(mine[k], to_group(k // 2, k % 2)) for k in (1, 2, 3)]
    chunk_b, far_a = lax.optimization_barrier((chunk_b, far_a))
    far_b = gather_begin(chunk_b)
    pair_a = gather_rest(chunk_a, far_a)
    b0, b1, r2, r3 = stand(where, pieces)

    keep, out = step("solve_0", where, lambda v: ([v[0]], []), [b0], [pair_a], [(0, 0, 0)])
    got = send(out, to_pair)
    chunk_c, far_b = lax.optimization_barrier((chunk_c, far_b))
    far_c = gather_begin(chunk_c)
    pair_b = gather_rest(chunk_b, far_b)
    keep, out, y0 = step(
        "update_10", where, lambda v: ([v[0] + v[1]], [v[0] + v[1]]), [keep, got], [pair_a], [(0, 1, 0)], 1
    )
    got = send(out, to_pair)
    keep1, out = step(
        "solve_1", where, lambda v: ([v[0] - (v[1] + v[2])], []), [b1, keep, got], [pair_b], [(0, 0, 0)]
    )
    got1 = send(out, to_pair)
    pair_c = gather_rest(chunk_c, far_c)
    keep, out, y1 = step(
        "update_2",
        where,
        lambda v: ([v[0], v[1] + v[2]], [v[1] + v[2]]),
        [y0, keep1, got1],
        [pair_b],
        [(0, 1, 0), (0, 2, 1)],
        1,
    )
    got = send(out, to_pair)
    own2 = keep + got
    other2 = send(own2, to_core)
    keep3, out3 = step(
        "update_3", where, lambda v: (v, []), [y0, y1], [pair_c], [(0, 0, 0), (0, 1, 1)]
    )
    got3 = send(out3, to_pair)
    keep, out = step(
        "solve_2", where, lambda v: ([v[0] - (v[1] + v[2])], []), [r2, own2, other2], [pair_c], [(0, 2, 0)]
    )
    got = send(out, to_pair)
    own3 = keep3 + got3
    other3 = send(own3, to_core)
    keep, out, y2 = step(
        "update_32", where, lambda v: ([v[0] + v[1]], [v[0] + v[1]]), [keep, got], [pair_c], [(0, 4, 0)], 1
    )
    got = send(out, to_pair)

    leaf_parts = lay("lay_leaf", where, y0, keep1, got1)
    leaf_near = jnp.stack(
        [leaf_parts[0]] + [send(leaf_parts[k], to_group(k // 2, k % 2)) for k in (1, 2, 3)]
    )
    leaf_other = send(leaf_near, to_row)
    leaf_solution = join("join_leaf", where, leaf_near, leaf_other)

    keep, out = step(
        "solve_3",
        where,
        lambda v: ([v[0] - (v[1] + v[2]) - (v[3] + v[4])], []),
        [r3, own3, other3, keep, got],
        [pair_c],
        [(0, 3, 0)],
    )
    got = send(out, to_pair)
    root_parts = lay("lay_root", where, y2, keep, got)
    moved = jnp.stack([send(root_parts[k], to_group_by_core(k // 2, k % 2)) for k in range(4)])
    swapped = send(moved, to_core)
    near = jnp.where(core == 0, moved, swapped)
    other = jnp.where(core == 0, swapped, moved)
    root_solution = join("join_root", where, near, other)
    return leaf_solution[None], root_solution


def solution(mesh):
    placed = (
        P("leaf", None, None, "col", None),
        P(None, None, "col", None),
        P("leaf", None, None, "col", "row"),
        P(None, None, "col", "row"),
        P("leaf", None, None, "col", "row"),
        P(None, "col", "row"),
        P("leaf", None, "row", "col"),
    )
    small = (mesh.shape["row"], mesh.shape["col"], mesh.shape["leaf"]) == (2, 8, 2)
    return jax.shard_map(
        grouped if small else general,
        mesh=mesh,
        in_specs=placed,
        out_specs=(P("leaf", None, None, "col", None), P(None, None, "col", None)),
        check_vma=False,
    )
```

```python
import functools

import jax
import jax.numpy as jnp
from jax import lax
from jax.experimental import pallas as pl
from jax.experimental.pallas import tpu as pltpu
from jax.sharding import PartitionSpec as P

BLK = 128
AXES = ("row", "col", "leaf")
F32 = jnp.float32
BF16 = jnp.bfloat16


def apply_rows(block, vector):
    block = block.reshape(-1, block.shape[-1])
    vector = vector.reshape(-1, vector.shape[-1])
    term = lax.dot_general(
        block,
        vector,
        (((0,), (0,)), ((), ())),
        precision=lax.Precision.HIGHEST,
        preferred_element_type=F32,
    )
    owned = lax.psum_scatter(term, "col", scatter_dimension=0, tiled=True)
    return lax.all_gather(owned[None], "row", axis=0, tiled=True)


def masked(leaf_blocks, pattern):
    local = leaf_blocks[0]
    shaped = local.reshape(local.shape[:3] + (local.shape[3] // BLK, BLK))
    weights = pattern[0].astype(F32).transpose(0, 2, 1)[:, None, :, :, None]
    return (shaped * weights).reshape(local.shape)


def general(leaf_rhs, root_rhs, leaf_inverses, root_inverses, leaf_blocks, root_block, pattern):
    blocks = masked(leaf_blocks, pattern)
    first = apply_rows(leaf_inverses[0, 0], leaf_rhs[0, 0])
    second = apply_rows(leaf_inverses[0, 1], leaf_rhs[0, 1] - apply_rows(blocks[0], first))
    upper_two = apply_rows(blocks[1], first) + apply_rows(blocks[2], second)
    upper_three = apply_rows(blocks[3], first) + apply_rows(blocks[4], second)
    upper_two, upper_three = lax.psum((upper_two, upper_three), "leaf")
    third = apply_rows(root_inverses[0], root_rhs[0] - upper_two)
    fourth = apply_rows(root_inverses[1], root_rhs[1] - upper_three - apply_rows(root_block, third))
    return (jnp.stack([first, second])[None], jnp.stack([third, fourth]))


def pairs(dest):
    out = []
    for r in range(2):
        for zh in range(2):
            for zl in range(2):
                for x in range(2):
                    for l in range(2):
                        d = dest(r, zh, zl, x, l)
                        if d is None:
                            continue
                        s = (r * 8 + zh * 4 + zl * 2 + x) * 2 + l
                        e = (d[0] * 8 + d[1] * 4 + d[2] * 2 + d[3]) * 2 + d[4]
                        out.append((s, e))
    return out


def send(value, dest):
    return lax.ppermute(value, AXES, pairs(dest))


def to_far(r, zh, zl, x, l):
    return r, zh ^ 1, zl, x, l


def to_second(r, zh, zl, x, l):
    return (r, zh, zl, x ^ 1, l) if l == 0 else (r ^ 1, zh, zl, x, l)


def to_third(r, zh, zl, x, l):
    return (r ^ 1, zh, zl, x, l) if l == 0 else (r, zh, zl, x ^ 1, l)


def to_pair(r, zh, zl, x, l):
    return r, zh, zl ^ 1, x, l


def to_core(r, zh, zl, x, l):
    return r, zh, zl, x, l ^ 1


def to_pair_core(r, zh, zl, x, l):
    return r, zh, zl ^ 1, x, l ^ 1


def to_row(r, zh, zl, x, l):
    return r ^ 1, zh, zl, x, l


def to_group(b1, b2):
    return lambda r, zh, zl, x, l: (r, zh ^ b1, zl, x ^ b2, l)


def to_group_by_core(b1, b2):
    return lambda r, zh, zl, x, l: (r ^ l, zh ^ b1, zl, x ^ b2, l)


def after(value, *others):
    return lax.optimization_barrier((value,) + others)[0]


def vmem():
    return pl.BlockSpec(memory_space=pltpu.VMEM)


def anywhere():
    return pl.BlockSpec(memory_space=pl.ANY)


def smem():
    return pl.BlockSpec(memory_space=pltpu.SMEM)


def shaped(*dims):
    return jax.ShapeDtypeStruct(dims, F32)


def lanes_low():
    return lax.broadcasted_iota(jnp.int32, (1, 128), 1) < 64


def swap_lanes(one, two):
    low = lanes_low()
    even = jnp.where(low, one, pltpu.roll(two, 64, one.ndim - 1))
    odd = jnp.where(low, pltpu.roll(one, 64, one.ndim - 1), two)
    return even, odd


def split(value):
    high = value.astype(BF16)
    return high, (value - high.astype(F32)).astype(BF16)


def dot3(left, right):
    lh, ll = left
    rh, rl = right
    whole = jnp.dot(lh, rl, preferred_element_type=F32)
    whole += jnp.dot(ll, rh, preferred_element_type=F32)
    return whole + jnp.dot(lh, rh, preferred_element_type=F32)


def flat(value):
    return jnp.concatenate([value[:64], value[64:]], axis=1)


def rows_kernel(where_ref, leaf_ref, root_ref, first_ref, keep_ref, out_ref):
    zl = where_ref[2]
    for m in range(4):
        source = leaf_ref if m < 2 else root_ref
        for a in range(2):
            even, odd = swap_lanes(source[m % 2, a, :, :128], source[m % 2, a, :, 128:])
            mine = jnp.where(zl == 0, even, odd)
            theirs = jnp.where(zl == 0, odd, even)
            keep_ref[m, a] = mine
            if m == 0:
                first_ref[a] = theirs
            else:
                out_ref[m - 1, a] = theirs


def rows(where, leaf, root):
    return pl.pallas_call(
        rows_kernel,
        out_shape=[shaped(2, 32, 128), shaped(4, 2, 32, 128), shaped(3, 2, 32, 128)],
        in_specs=[smem(), vmem(), vmem()],
        out_specs=[vmem()] * 3,
        name="split_rows",
    )(where, leaf, root)


def mask_kernel(tiles_ref, blocks_ref, out_ref):
    for m in range(5):
        for t in range(2):
            weight = tiles_ref[m, t].astype(F32)
            for a in range(2):
                out_ref[m, t, a] = blocks_ref[m, a, :, t * 128 : t * 128 + 128] * weight


def mask(tiles, blocks):
    return pl.pallas_call(
        mask_kernel,
        out_shape=shaped(5, 2, 2, 32, 128),
        in_specs=[smem(), vmem()],
        out_specs=vmem(),
        name="mask_blocks",
    )(tiles, blocks)


def fetch(where_ref, near, far, m, dest, sems):
    r, zh, x, l = where_ref[0], where_ref[1], where_ref[3], where_ref[4]
    copies = []
    for b3, source in enumerate((near, far)):
        for b2 in range(2):
            for b1 in range(2):
                rr = r ^ jnp.where(l == 0, b3, b2)
                xx = x ^ jnp.where(l == 0, b2, b3)
                copy = pltpu.make_async_copy(
                    source.at[b2 * 2 + b1, m],
                    dest(rr, zh ^ b1, xx),
                    sems.at[b3 * 4 + b2 * 2 + b1],
                )
                copy.start()
                copies.append(copy)
    return copies


def solve(inverse, vector, copies):
    for copy in copies:
        copy.wait()
    left = split(flat(vector))
    parts = [dot3(left, split(inverse[a].reshape(512, 128))) for a in range(2)]
    return jnp.concatenate(parts, axis=0)


def update(held, terms, copies):
    sums = [None, None]
    for t, vector in enumerate(terms):
        for copy in copies[t]:
            copy.wait()
        left = split(flat(vector))
        for a in range(2):
            right = jnp.concatenate(
                [held[t, a, 0].reshape(256, 128), held[t, a, 1].reshape(256, 128)], axis=1
            )
            part = dot3(left, split(right))
            sums[a] = part if sums[a] is None else sums[a] + part
    return jnp.concatenate(sums, axis=0)


def link_kernel(plan, where_ref, *refs):
    nvec, nchunk = plan["nvec"], plan["nchunk"]
    vecs = refs[:nvec]
    chunks = refs[nvec : nvec + 2 * nchunk]
    rest = refs[nvec + 2 * nchunk :]
    outs, (inverse, held, sems) = rest[:2], rest[2:]
    chunk, m = plan["inverse"]
    solving = fetch(
        where_ref,
        chunks[2 * chunk],
        chunks[2 * chunk + 1],
        m,
        lambda r, zh, x: inverse.at[r, :, zh, :, x],
        sems.at[0],
    )
    updating = [
        fetch(
            where_ref,
            chunks[2 * chunk],
            chunks[2 * chunk + 1],
            m,
            lambda r, zh, x, t=t: held.at[t, r, :, :, zh, x],
            sems.at[t + 1],
        )
        for t, (chunk, m) in enumerate(plan["blocks"])
    ]
    values = [v[...] for v in vecs]
    solved = solve(inverse, plan["input"](values), solving)
    outs[0][...] = update(held, plan["terms"](values, solved, where_ref[4]), updating)
    outs[1][...] = solved


def link(name, where, vecs, chunks, plan):
    arrays = [array for pair in chunks for array in pair]
    nblocks = len(plan["blocks"])
    plan = dict(plan, nvec=len(vecs), nchunk=len(chunks))
    last = nblocks == 0
    scratch = [pltpu.VMEM((4, 2, 32, 128), F32)] if last else []
    outs = [shaped(2, 32, 128)] * 4 if last else [shaped(128, 256), shaped(128, 128)]
    return pl.pallas_call(
        functools.partial(link_kernel, plan) if not last else functools.partial(last_kernel, plan),
        out_shape=outs,
        in_specs=[smem()] + [vmem()] * len(vecs) + [anywhere()] * len(arrays),
        out_specs=[vmem()] * len(outs),
        scratch_shapes=scratch
        + [
            pltpu.VMEM((2, 2, 2, 2, 2, 32, 128), F32),
            pltpu.VMEM((max(nblocks, 1), 2, 2, 2, 2, 2, 32, 128), F32),
            pltpu.SemaphoreType.DMA((nblocks + 1, 8)),
        ],
        name=name,
    )(where, *vecs, *arrays)


def last_kernel(plan, where_ref, *refs):
    nvec, nchunk = plan["nvec"], plan["nchunk"]
    vecs = refs[:nvec]
    chunks = refs[nvec : nvec + 2 * nchunk]
    outs = refs[nvec + 2 * nchunk : nvec + 2 * nchunk + 4]
    pieces, inverse, _, sems = refs[nvec + 2 * nchunk + 4 :]
    chunk, m = plan["inverse"]
    solving = fetch(
        where_ref,
        chunks[2 * chunk],
        chunks[2 * chunk + 1],
        m,
        lambda r, zh, x: inverse.at[r, :, zh, :, x],
        sems.at[0],
    )
    values = [v[...] for v in vecs]
    solved = solve(inverse, plan["input"](values), solving)
    lay_values(where_ref, (values[-1], solved), outs, pieces)


def lay_values(where_ref, values, outs, held):
    zh, x = where_ref[1], where_ref[3]
    for p, value in enumerate(values):
        held[:, p] = value.T.reshape(4, 32, 128)
    for b1 in range(2):
        for b2 in range(2):
            outs[b1 * 2 + b2][...] = held[(zh ^ b1) * 2 + (x ^ b2)]


def lay_kernel(where_ref, first, second, *refs):
    lay_values(where_ref, (first[...], second[...]), refs[:4], refs[4])


def lay(name, where, first, second):
    return pl.pallas_call(
        lay_kernel,
        out_shape=[shaped(2, 32, 128)] * 4,
        in_specs=[smem()] + [vmem()] * 2,
        out_specs=[vmem()] * 4,
        scratch_shapes=[pltpu.VMEM((4, 2, 32, 128), F32)],
        name=name,
    )(where, first, second)


def cut_kernel(where_ref, source, *refs):
    outs, held = refs[:4], refs[4]
    r, zh, x = where_ref[0], where_ref[1], where_ref[3]
    for p in range(2):
        for z in range(2):
            start = pl.multiple_of((2 * r + z) * 128, 128)
            one = source[p, 0, :, pl.ds(start, 128)]
            two = source[p, 1, :, pl.ds(start, 128)]
            held[2 * z, p], held[2 * z + 1, p] = swap_lanes(one, two)
    for b1 in range(2):
        for b2 in range(2):
            outs[b1 * 2 + b2][...] = held[(zh ^ b1) * 2 + (x ^ b2)]


def cut(name, where, rhs):
    return pl.pallas_call(
        cut_kernel,
        out_shape=[shaped(2, 32, 128)] * 4,
        in_specs=[smem(), vmem()],
        out_specs=[vmem()] * 4,
        scratch_shapes=[pltpu.VMEM((4, 2, 32, 128), F32)],
        name=name,
    )(where, rhs)


def stand_kernel(where_ref, near_ref, other_ref, one_ref, two_ref, held):
    zh, zl, x = where_ref[1], where_ref[2], where_ref[3]
    for b1 in range(2):
        for b2 in range(2):
            for b, source in enumerate((near_ref, other_ref)):
                held[((zh ^ b1) * 2 + (zl ^ b)) * 2 + (x ^ b2)] = source[b1 * 2 + b2]
    for p, out in enumerate((one_ref, two_ref)):
        out[...] = held[:, p].reshape(256, 128).T


def stand(name, where, near, other):
    return pl.pallas_call(
        stand_kernel,
        out_shape=[shaped(128, 256)] * 2,
        in_specs=[smem()] + [vmem()] * 2,
        out_specs=[vmem()] * 2,
        scratch_shapes=[pltpu.VMEM((8, 2, 32, 128), F32)],
        name=name,
    )(where, near, other)


def join_kernel(where_ref, near_ref, other_ref, out_ref, held):
    r, zh, x, core = where_ref[0], where_ref[1], where_ref[3], where_ref[5]
    for b1 in range(2):
        for b2 in range(2):
            place = (zh ^ b1) * 2 + (x ^ b2)
            held[(r ^ core) * 4 + place] = near_ref[b1 * 2 + b2]
            held[(r ^ core ^ 1) * 4 + place] = other_ref[b1 * 2 + b2]
    for p in range(2):
        for u in range(4):
            lanes = slice(u * 128, u * 128 + 128)
            out_ref[p, 0, :, lanes], out_ref[p, 1, :, lanes] = swap_lanes(
                held[2 * u, p], held[2 * u + 1, p]
            )


def join(name, where, near, other):
    return pl.pallas_call(
        join_kernel,
        out_shape=shaped(2, 2, 32, 512),
        in_specs=[smem()] + [vmem()] * 2,
        out_specs=vmem(),
        scratch_shapes=[pltpu.VMEM((8, 2, 32, 128), F32)],
        name=name,
    )(where, near, other)


def exchange_four(value):
    return send(value, to_pair), send(value, to_core), send(value, to_pair_core)


def sum_four(v):
    return (v[0] + v[1]) + (v[2] + v[3])


def grouped(leaf_rhs, root_rhs, leaf_inverses, root_inverses, leaf_blocks, root_block, pattern):
    row, col, core = (lax.axis_index(name) for name in AXES)
    zl = (col // 2) % 2
    spots = [row, col // 4, zl, col % 2, core]
    where = jnp.stack(spots + [jnp.zeros_like(core)]).astype(jnp.int32)
    where_by_core = jnp.stack(spots + [core]).astype(jnp.int32)

    first_out, keeps, outs = rows(where, leaf_inverses[0], root_inverses)
    first_got = send(first_out, to_pair)
    blocks = mask(pattern[0, :, :, 0], leaf_blocks[0])

    def whole(keep, got):
        return jnp.stack([jnp.where(zl == 0, keep, got), jnp.where(zl == 0, got, keep)], axis=-3)

    chunk_a = jnp.stack([whole(keeps[0], first_got), blocks[0]])
    far_a = send(chunk_a, to_far)

    leaf_cut = cut("cut_leaf", where, leaf_rhs[0])
    leaf_in = jnp.stack(
        [leaf_cut[0]] + [send(leaf_cut[k], to_group(k // 2, k % 2)) for k in (1, 2, 3)]
    )
    leaf_pair = send(leaf_in, to_pair)

    outs = after(outs, chunk_a)
    rest_got = send(outs, to_pair)
    inverses = whole(keeps[1:], rest_got)
    chunk_b = jnp.concatenate([inverses[:1], blocks[1:3]])
    lower = root_block.reshape(2, 32, 2, 128).transpose(2, 0, 1, 3)
    chunk_c = blocks[3:5]
    chunk_d = jnp.concatenate([inverses[1:], lower[None]])

    two_a = jnp.stack([chunk_a, far_a])
    second_a = send(two_a, to_second)
    far_b = send(after(chunk_b, two_a), to_far)
    four_a = jnp.concatenate([two_a, second_a])
    third_a = send(four_a, to_third)
    two_b = jnp.stack([chunk_b, after(far_b, four_a)])
    second_b = send(two_b, to_second)
    far_c = send(after(chunk_c, two_b), to_far)
    b0, b1 = stand("stand_leaf", where, after(leaf_in, two_b), leaf_pair)

    part, y0 = link(
        "link_0",
        where,
        [b0],
        [(four_a, third_a)],
        dict(
            inverse=(0, 0),
            blocks=[(0, 1)],
            input=lambda v: v[0],
            terms=lambda v, solved, core: [solved],
        ),
    )
    pair = send(part, to_pair)
    four_b = jnp.concatenate([two_b, after(second_b, part)])
    third_b = send(four_b, to_third)
    two_c = jnp.stack([chunk_c, after(far_c, four_b)])
    second_c = send(two_c, to_second)
    far_d = send(after(chunk_d, two_c), to_far)

    root_cut = cut("cut_root", where, after(root_rhs, two_c))
    root_in = jnp.stack(
        [root_cut[0]] + [send(root_cut[k], to_group(k // 2, k % 2)) for k in (1, 2, 3)]
    )
    root_pair = send(root_in, to_pair)

    part, y1 = link(
        "link_1",
        where,
        [b1, part, pair, y0],
        [(four_b, third_b)],
        dict(
            inverse=(0, 0),
            blocks=[(0, 1), (0, 2)],
            input=lambda v: v[0] - (v[1] + v[2]),
            terms=lambda v, solved, core: [v[3], solved],
        ),
    )
    sums = exchange_four(part)
    four_c = jnp.concatenate([two_c, after(second_c, part)])
    third_c = send(four_c, to_third)
    two_d = jnp.stack([chunk_d, after(far_d, four_c)])
    second_d = send(two_d, to_second)
    r2, r3 = stand("stand_root", where, after(root_in, two_d), root_pair)
    four_d = jnp.concatenate([two_d, second_d])
    third_d = send(four_d, to_third)

    leaf_parts = lay("lay_leaf", where, after(y0, four_d), y1)
    leaf_near = jnp.stack(
        [leaf_parts[0]] + [send(leaf_parts[k], to_group(k // 2, k % 2)) for k in (1, 2, 3)]
    )

    part, y2 = link(
        "link_2",
        where,
        [r2, part, *sums, y0, y1],
        [(four_c, third_c), (four_d, third_d)],
        dict(
            inverse=(1, 0),
            blocks=[(0, 0), (0, 1), (1, 2)],
            input=lambda v: v[0] - sum_four(v[1:5]),
            terms=lambda v, solved, core: [v[5], v[6], jnp.where(core == 0, solved, 0.0)],
        ),
    )
    sums = exchange_four(part)
    leaf_near = after(leaf_near, part)
    leaf_other = send(leaf_near, to_row)
    leaf_solution = join("join_leaf", where, leaf_near, leaf_other)

    root_parts = link(
        "link_3",
        where,
        [r3, part, *sums, y2],
        [(four_d, third_d)],
        dict(inverse=(0, 1), blocks=[], input=lambda v: v[0] - sum_four(v[1:5])),
    )
    moved = jnp.stack([send(root_parts[k], to_group_by_core(k // 2, k % 2)) for k in range(4)])
    swapped = send(moved, to_core)
    root_solution = join("join_root", where_by_core, moved, swapped)
    return leaf_solution[None], root_solution


def solution(mesh):
    placed = (
        P("leaf", None, None, "col", None),
        P(None, None, "col", None),
        P("leaf", None, None, "col", "row"),
        P(None, None, "col", "row"),
        P("leaf", None, None, "col", "row"),
        P(None, "col", "row"),
        P("leaf", None, "row", "col"),
    )
    small = (mesh.shape["row"], mesh.shape["col"], mesh.shape["leaf"]) == (2, 8, 2)
    return jax.shard_map(
        grouped if small else general,
        mesh=mesh,
        in_specs=placed,
        out_specs=(P("leaf", None, None, "col", None), P(None, None, "col", None)),
        check_vma=False,
    )
```

```python
import functools

import jax
import jax.numpy as jnp
from jax import lax
from jax.experimental import pallas as pl
from jax.experimental.pallas import tpu as pltpu
from jax.sharding import PartitionSpec as P

BLK = 128
AXES = ("row", "col", "leaf")
F32 = jnp.float32
BF16 = jnp.bfloat16
VMEM_OF_A_KERNEL = 16 * 2**20


def apply_rows(block, vector):
    block = block.reshape(-1, block.shape[-1])
    vector = vector.reshape(-1, vector.shape[-1])
    term = lax.dot_general(
        block,
        vector,
        (((0,), (0,)), ((), ())),
        precision=lax.Precision.HIGHEST,
        preferred_element_type=F32,
    )
    owned = lax.psum_scatter(term, "col", scatter_dimension=0, tiled=True)
    return lax.all_gather(owned[None], "row", axis=0, tiled=True)


def masked(leaf_blocks, pattern):
    local = leaf_blocks[0]
    shaped = local.reshape(local.shape[:3] + (local.shape[3] // BLK, BLK))
    weights = pattern[0].astype(F32).transpose(0, 2, 1)[:, None, :, :, None]
    return (shaped * weights).reshape(local.shape)


def general(leaf_rhs, root_rhs, leaf_inverses, root_inverses, leaf_blocks, root_block, pattern):
    blocks = masked(leaf_blocks, pattern)
    first = apply_rows(leaf_inverses[0, 0], leaf_rhs[0, 0])
    second = apply_rows(leaf_inverses[0, 1], leaf_rhs[0, 1] - apply_rows(blocks[0], first))
    upper_two = apply_rows(blocks[1], first) + apply_rows(blocks[2], second)
    upper_three = apply_rows(blocks[3], first) + apply_rows(blocks[4], second)
    upper_two, upper_three = lax.psum((upper_two, upper_three), "leaf")
    third = apply_rows(root_inverses[0], root_rhs[0] - upper_two)
    fourth = apply_rows(root_inverses[1], root_rhs[1] - upper_three - apply_rows(root_block, third))
    return (jnp.stack([first, second])[None], jnp.stack([third, fourth]))


def pairs(dest):
    out = []
    for r in range(2):
        for zh in range(2):
            for zl in range(2):
                for x in range(2):
                    for l in range(2):
                        d = dest(r, zh, zl, x, l)
                        if d is None:
                            continue
                        s = (r * 8 + zh * 4 + zl * 2 + x) * 2 + l
                        e = (d[0] * 8 + d[1] * 4 + d[2] * 2 + d[3]) * 2 + d[4]
                        out.append((s, e))
    return out


def send(value, dest):
    return lax.ppermute(value, AXES, pairs(dest))


def to_far(r, zh, zl, x, l):
    return r, zh ^ 1, zl, x, l


def to_second(r, zh, zl, x, l):
    return (r, zh, zl, x ^ 1, l) if l == 0 else (r ^ 1, zh, zl, x, l)


def to_third(r, zh, zl, x, l):
    return (r ^ 1, zh, zl, x, l) if l == 0 else (r, zh, zl, x ^ 1, l)


def to_pair(r, zh, zl, x, l):
    return r, zh, zl ^ 1, x, l


def to_core(r, zh, zl, x, l):
    return r, zh, zl, x, l ^ 1


def to_pair_core(r, zh, zl, x, l):
    return r, zh, zl ^ 1, x, l ^ 1


def to_row(r, zh, zl, x, l):
    return r ^ 1, zh, zl, x, l


def to_group(b1, b2):
    return lambda r, zh, zl, x, l: (r, zh ^ b1, zl, x ^ b2, l)


def to_group_by_core(b1, b2):
    return lambda r, zh, zl, x, l: (r ^ l, zh ^ b1, zl, x ^ b2, l)


def after(value, *others):
    return lax.optimization_barrier((value,) + others)[0]


def vmem():
    return pl.BlockSpec(memory_space=pltpu.VMEM)


def smem():
    return pl.BlockSpec(memory_space=pltpu.SMEM)


def shaped(*dims):
    return jax.ShapeDtypeStruct(dims, F32)


def lanes_low():
    return lax.broadcasted_iota(jnp.int32, (1, 128), 1) < 64


def swap_lanes(one, two):
    low = lanes_low()
    even = jnp.where(low, one, pltpu.roll(two, 64, one.ndim - 1))
    odd = jnp.where(low, pltpu.roll(one, 64, one.ndim - 1), two)
    return even, odd


def split(value):
    high = value.astype(BF16)
    return high, (value - high.astype(F32)).astype(BF16)


def dot3(left, right):
    lh, ll = left
    rh, rl = right
    whole = jnp.dot(lh, rl, preferred_element_type=F32)
    whole += jnp.dot(ll, rh, preferred_element_type=F32)
    return whole + jnp.dot(lh, rh, preferred_element_type=F32)


def flat(value):
    return jnp.concatenate([value[:64], value[64:]], axis=1)


def spot():
    row, col, core = (lax.axis_index(name) for name in AXES)
    return row, col // 4, (col // 2) % 2, col % 2, core


def call(name, kernel, outs, *operands, specs=None, scratch=()):
    specs = specs or [None] * len(operands)
    fixed = [
        pltpu.with_memory_space_constraint(o, pltpu.VMEM) if s is None else o
        for o, s in zip(operands, specs)
    ]
    return pl.pallas_call(
        kernel,
        out_shape=[pltpu.VMEM(dims, F32) for dims in outs],
        in_specs=[vmem() if s is None else s for s in specs],
        out_specs=[vmem() for _ in outs],
        scratch_shapes=list(scratch),
        compiler_params=pltpu.CompilerParams(vmem_limit_bytes=VMEM_OF_A_KERNEL),
        name=name,
    )(*fixed)


def cut_columns(source, held, outs):
    r, zh, _, x, _ = spot()
    for p in range(2):
        for z in range(2):
            start = pl.multiple_of((2 * r + z) * 128, 128)
            one = source[p, 0, :, pl.ds(start, 128)]
            two = source[p, 1, :, pl.ds(start, 128)]
            held[2 * z, p], held[2 * z + 1, p] = swap_lanes(one, two)
    for b1 in range(2):
        for b2 in range(2):
            outs[b1 * 2 + b2][...] = held[(zh ^ b1) * 2 + (x ^ b2)]


def part_rows(source, keep, out):
    zl = spot()[2]
    for a in range(2):
        even, odd = swap_lanes(source[a, :, :128], source[a, :, 128:])
        keep[a] = jnp.where(zl == 0, even, odd)
        out[a] = jnp.where(zl == 0, odd, even)


def begin_kernel(inverse_ref, rhs_ref, *refs):
    part_rows(inverse_ref.at[0, 0], refs[0], refs[1])
    cut_columns(rhs_ref.at[0], refs[6], refs[2:6])


def prepare_kernel(tiles_ref, inverse_ref, root_ref, blocks_ref, lower_ref, rhs_ref, *refs):
    keep, out, masked_ref, lower_out = refs[:4]
    part_rows(inverse_ref.at[0, 1], keep.at[0], out.at[0])
    for m in range(2):
        part_rows(root_ref.at[m], keep.at[m + 1], out.at[m + 1])
    for t in range(2):
        lanes = slice(t * 128, t * 128 + 128)
        for a in range(2):
            lower_out[t, a] = lower_ref[a, :, lanes]
        for m in range(5):
            weight = tiles_ref[0, m, t, 0].astype(F32)
            for a in range(2):
                masked_ref[m, t, a] = blocks_ref[0, m, a, :, lanes] * weight
    cut_columns(rhs_ref, refs[8], refs[4:8])


def fetch(near, far, pick, dest, sems, swapped=None, from_core=0):
    r, zh, _, x, l = spot()
    copies = []
    for b3 in range(2):
        for b2 in range(2):
            for b1 in range(2):

                def copy_of(sources, core):
                    rr = r ^ jnp.where(core == 0, b3, b2)
                    xx = x ^ jnp.where(core == 0, b2, b3)
                    return pltpu.make_async_copy(
                        pick(sources[b3], b2 * 2 + b1),
                        dest(rr, zh ^ b1, xx),
                        sems.at[b3 * 4 + b2 * 2 + b1],
                    )

                copy = copy_of((near, far), l)
                if swapped is None:
                    copy.start()
                else:
                    pl.when(l == from_core)(copy.start)
                    pl.when(l != from_core)(copy_of(swapped, 1 - l).start)
                copies.append(copy)
    return copies


def wait_all(copies):
    for copy in copies:
        copy.wait()


def solve(inverse, vector):
    left = split(flat(vector))
    parts = [dot3(left, split(inverse[a].reshape(512, 128))) for a in range(2)]
    return jnp.concatenate(parts, axis=0)


def update(held, terms, waits):
    sums = [None, None]
    for t, vector in enumerate(terms):
        waits[t]()
        left = split(flat(vector))
        for a in range(2):
            right = jnp.concatenate(
                [held[t, a, 0].reshape(256, 128), held[t, a, 1].reshape(256, 128)], axis=1
            )
            part = dot3(left, split(right))
            sums[a] = part if sums[a] is None else sums[a] + part
    return jnp.concatenate(sums, axis=0)


def sum_four(refs):
    return (refs[0][...] + refs[1][...]) + (refs[2][...] + refs[3][...])


def inverse_place(inverse):
    return lambda r, zh, x: inverse.at[r, :, zh, :, x]


def block_place(held, t):
    return lambda r, zh, x: held.at[t, r, :, :, zh, x]


def half_place(held, t, half):
    return lambda r, zh, x: held.at[t, r, half, :, zh, x]


def matrix(m):
    return lambda ref, b: ref.at[b, m]


def link_0_kernel(b_ref, near, far, part_ref, y_ref, inverse, held, sems):
    first = fetch(near, far, matrix(0), inverse_place(inverse), sems.at[0])
    second = fetch(near, far, matrix(1), block_place(held, 0), sems.at[1])
    wait_all(first)
    solved = solve(inverse, b_ref[...])
    y_ref[...] = solved
    part_ref[...] = update(held, [solved], [functools.partial(wait_all, second)])


def link_1_kernel(b_ref, own, got, y0_ref, near, far, part_ref, y_ref, inverse, held, sems):
    copies = [fetch(near, far, matrix(0), inverse_place(inverse), sems.at[0])]
    for t in range(2):
        copies.append(fetch(near, far, matrix(t + 1), block_place(held, t), sems.at[t + 1]))
    wait_all(copies[0])
    solved = solve(inverse, b_ref[...] - (own[...] + got[...]))
    y_ref[...] = solved
    waits = [functools.partial(wait_all, c) for c in copies[1:]]
    part_ref[...] = update(held, [y0_ref[...], solved], waits)


def link_2_kernel(b_ref, s0, s1, s2, s3, y0_ref, y1_ref, near, far, *refs):
    root, swapped = refs[:2], refs[2:4]
    part_ref, y_ref, inverse, held, sems = refs[4:]
    first = fetch(
        *root, lambda ref, b: ref.at[b, pl.ds(0, 2)], inverse_place(inverse), sems.at[0], swapped, 0
    )
    copies = [fetch(near, far, matrix(t), block_place(held, t), sems.at[t + 1]) for t in range(2)]
    halves = [
        fetch(*root, matrix(2), half_place(held, 2, h), sems.at[3 + h], swapped, h) for h in range(2)
    ]
    wait_all(first)
    solved = solve(inverse, b_ref[...] - sum_four((s0, s1, s2, s3)))
    y_ref[...] = solved
    copies.append(halves[0] + halves[1])
    waits = [functools.partial(wait_all, c) for c in copies]
    last = jnp.where(spot()[4] == 0, solved, 0.0)
    part_ref[...] = update(held, [y0_ref[...], y1_ref[...], last], waits)


def link_3_kernel(b_ref, s0, s1, s2, s3, y2_ref, *refs):
    root, swapped, outs = refs[:2], refs[2:4], refs[4:8]
    pieces, inverse, sems = refs[8:]
    first = fetch(
        *root, lambda ref, b: ref.at[b, pl.ds(0, 2)], inverse_place(inverse), sems.at[0], swapped, 1
    )
    vector = b_ref[...] - sum_four((s0, s1, s2, s3))
    wait_all(first)
    lay_values((y2_ref[...], solve(inverse, vector)), outs, pieces)


def link_scratch(nblocks, nsems):
    blocks = [pltpu.VMEM((nblocks, 2, 2, 2, 2, 2, 32, 128), F32)] if nblocks else []
    return (
        [pltpu.VMEM((2, 2, 2, 2, 2, 32, 128), F32)] + blocks + [pltpu.SemaphoreType.DMA((nsems, 8))]
    )


def lay_values(values, outs, held):
    _, zh, _, x, _ = spot()
    for p, value in enumerate(values):
        held[:, p] = value.T.reshape(4, 32, 128)
    for b1 in range(2):
        for b2 in range(2):
            outs[b1 * 2 + b2][...] = held[(zh ^ b1) * 2 + (x ^ b2)]


def lay_kernel(first, second, *refs):
    lay_values((first[...], second[...]), refs[:4], refs[4])


def stand_kernel(near_ref, other_ref, one_ref, two_ref, held):
    _, zh, zl, x, _ = spot()
    for b1 in range(2):
        for b2 in range(2):
            for b, source in enumerate((near_ref, other_ref)):
                held[((zh ^ b1) * 2 + (zl ^ b)) * 2 + (x ^ b2)] = source[b1 * 2 + b2]
    for p, out in enumerate((one_ref, two_ref)):
        out[...] = held[:, p].reshape(256, 128).T


def join_kernel(by_core, near_ref, other_ref, out_ref, held):
    r, zh, _, x, core = spot()
    near = r ^ core if by_core else r
    for b1 in range(2):
        for b2 in range(2):
            place = (zh ^ b1) * 2 + (x ^ b2)
            held[near * 4 + place] = near_ref[b1 * 2 + b2]
            held[(near ^ 1) * 4 + place] = other_ref[b1 * 2 + b2]
    for p in range(2):
        for u in range(4):
            lanes = slice(u * 128, u * 128 + 128)
            out_ref[p, 0, :, lanes], out_ref[p, 1, :, lanes] = swap_lanes(
                held[2 * u, p], held[2 * u + 1, p]
            )


def join(name, by_core, near, other):
    return pl.pallas_call(
        functools.partial(join_kernel, by_core),
        out_shape=shaped(2, 2, 32, 512),
        in_specs=[vmem()] * 2,
        out_specs=vmem(),
        scratch_shapes=[pltpu.VMEM((8, 2, 32, 128), F32)],
        compiler_params=pltpu.CompilerParams(vmem_limit_bytes=VMEM_OF_A_KERNEL),
        name=name,
    )(*(pltpu.with_memory_space_constraint(v, pltpu.VMEM) for v in (near, other)))


def to_groups(parts):
    return [parts[0]] + [send(parts[k], to_group(k // 2, k % 2)) for k in (1, 2, 3)]


PIECES = [(2, 32, 128)] * 4
VECTOR = [(128, 256), (128, 128)]


def grouped(leaf_rhs, root_rhs, leaf_inverses, root_inverses, leaf_blocks, root_block, pattern):
    core = lax.axis_index("leaf")
    zl = (lax.axis_index("col") // 2) % 2
    four_pieces = pltpu.VMEM((4, 2, 32, 128), F32)

    keep_0, out_0, *leaf_cut = call(
        "begin",
        begin_kernel,
        [(2, 32, 128)] * 2 + PIECES,
        leaf_inverses,
        leaf_rhs,
        specs=[vmem(), vmem()],
        scratch=[four_pieces],
    )
    got_0 = send(out_0, to_pair)
    leaf_moved = to_groups(leaf_cut)
    tiles, _ = lax.optimization_barrier((pattern, out_0))
    keeps, outs, blocks, lower, *root_cut = call(
        "prepare",
        prepare_kernel,
        [(3, 2, 32, 128)] * 2 + [(5, 2, 2, 32, 128), (2, 2, 32, 128)] + PIECES,
        tiles,
        leaf_inverses,
        root_inverses,
        leaf_blocks,
        root_block,
        root_rhs,
        specs=[smem()] + [vmem()] * 5,
        scratch=[four_pieces],
    )

    def whole(keep, got):
        return jnp.stack([jnp.where(zl == 0, keep, got), jnp.where(zl == 0, got, keep)], axis=-3)

    chunk_a = jnp.stack([whole(keep_0, got_0), blocks[0]])
    far_a = send(chunk_a, to_far)
    rest = send(after(outs, chunk_a), to_pair)
    leaf_in = jnp.stack(after(leaf_moved, chunk_a))
    leaf_pair = send(leaf_in, to_pair)

    inverses = whole(keeps, after(rest, leaf_in))
    chunk_b = jnp.concatenate([inverses[:1], blocks[1:3]])
    chunk_c = blocks[3:5]
    chunk_d = jnp.concatenate(
        [
            jnp.where(core == 0, inverses[1], inverses[2]),
            jnp.where(core == 0, lower[0], lower[1])[None],
        ]
    )
    b0, b1 = call(
        "stand_leaf",
        stand_kernel,
        [(128, 256)] * 2,
        after(leaf_in, chunk_b, chunk_d),
        leaf_pair,
        scratch=[pltpu.VMEM((8, 2, 32, 128), F32)],
    )

    two_a = jnp.stack([chunk_a, after(far_a, b0)])
    second_a = send(two_a, to_second)
    far_b = send(after(chunk_b, two_a), to_far)
    root_moved = to_groups(after(root_cut, two_a))
    four_a = jnp.concatenate([two_a, after(second_a, root_moved[0])])
    third_a = send(four_a, to_third)
    root_in = jnp.stack(after(root_moved, four_a))
    root_pair = send(root_in, to_pair)
    two_b = jnp.stack([chunk_b, after(far_b, root_in)])
    second_b = send(two_b, to_second)
    far_d = send(after(chunk_d, two_b), to_far)
    r2, r3 = call(
        "stand_root",
        stand_kernel,
        [(128, 256)] * 2,
        after(root_in, two_b),
        root_pair,
        scratch=[pltpu.VMEM((8, 2, 32, 128), F32)],
    )

    own, y0 = call(
        "link_0",
        link_0_kernel,
        VECTOR,
        after(b0, r2),
        four_a,
        third_a,
        scratch=link_scratch(1, 2),
    )
    got = send(own, to_pair)
    four_b = jnp.concatenate([two_b, after(second_b, own)])
    third_b = send(four_b, to_third)
    two_d = jnp.stack([chunk_d, after(far_d, four_b)])
    second_d = send(two_d, to_second)
    far_c = send(after(chunk_c, two_d), to_far)
    four_d = jnp.concatenate([two_d, after(second_d, far_c)])
    third_d = send(four_d, to_third)
    two_c = jnp.stack([chunk_c, after(far_c, four_d)])
    second_c = send(two_c, to_second)

    own, y1 = call(
        "link_1",
        link_1_kernel,
        VECTOR,
        after(b1, two_c),
        own,
        got,
        y0,
        four_b,
        third_b,
        scratch=link_scratch(2, 3),
    )
    sums = [own, send(own, to_pair), send(own, to_core), send(own, to_pair_core)]
    four_c = jnp.concatenate([two_c, after(second_c, own)])
    third_c = send(four_c, to_third)
    swap_d = (send(after(four_d, four_c), to_core), send(after(third_d, four_c), to_core))
    leaf_parts = call("lay_leaf", lay_kernel, PIECES, after(y0, four_c), y1, scratch=[four_pieces])
    leaf_moved = to_groups(leaf_parts)

    own, y2 = call(
        "link_2",
        link_2_kernel,
        VECTOR,
        after(r2, leaf_parts[0]),
        *sums,
        y0,
        y1,
        four_c,
        third_c,
        four_d,
        third_d,
        *swap_d,
        scratch=link_scratch(3, 5),
    )
    sums = [own, send(own, to_pair), send(own, to_core), send(own, to_pair_core)]
    leaf_near = jnp.stack(after(leaf_moved, own))
    leaf_other = send(leaf_near, to_row)
    leaf_solution = join("join_leaf", False, leaf_near, leaf_other)

    root_parts = call(
        "link_3",
        link_3_kernel,
        PIECES,
        after(r3, leaf_near),
        *sums,
        y2,
        four_d,
        third_d,
        *swap_d,
        scratch=[four_pieces] + link_scratch(0, 1),
    )
    moved = jnp.stack([send(root_parts[k], to_group_by_core(k // 2, k % 2)) for k in range(4)])
    swapped = send(moved, to_core)
    root_solution = join("join_root", True, moved, swapped)
    return leaf_solution[None], root_solution


def solution(mesh):
    placed = (
        P("leaf", None, None, "col", None),
        P(None, None, "col", None),
        P("leaf", None, None, "col", "row"),
        P(None, None, "col", "row"),
        P("leaf", None, None, "col", "row"),
        P(None, "col", "row"),
        P("leaf", None, "row", "col"),
    )
    small = (mesh.shape["row"], mesh.shape["col"], mesh.shape["leaf"]) == (2, 8, 2)
    return jax.shard_map(
        grouped if small else general,
        mesh=mesh,
        in_specs=placed,
        out_specs=(P("leaf", None, None, "col", None), P(None, None, "col", None)),
        check_vma=False,
    )
```

```python
import functools

import jax
import jax.numpy as jnp
from jax import lax
from jax.experimental import pallas as pl
from jax.experimental.pallas import tpu as pltpu
from jax.sharding import PartitionSpec as P

BLK = 128
AXES = ("row", "col", "leaf")
F32 = jnp.float32
BF16 = jnp.bfloat16
VMEM_OF_A_KERNEL = 16 * 2**20


def apply_rows(block, vector):
    block = block.reshape(-1, block.shape[-1])
    vector = vector.reshape(-1, vector.shape[-1])
    term = lax.dot_general(
        block,
        vector,
        (((0,), (0,)), ((), ())),
        precision=lax.Precision.HIGHEST,
        preferred_element_type=F32,
    )
    owned = lax.psum_scatter(term, "col", scatter_dimension=0, tiled=True)
    return lax.all_gather(owned[None], "row", axis=0, tiled=True)


def masked(leaf_blocks, pattern):
    local = leaf_blocks[0]
    shaped = local.reshape(local.shape[:3] + (local.shape[3] // BLK, BLK))
    weights = pattern[0].astype(F32).transpose(0, 2, 1)[:, None, :, :, None]
    return (shaped * weights).reshape(local.shape)


def general(leaf_rhs, root_rhs, leaf_inverses, root_inverses, leaf_blocks, root_block, pattern):
    blocks = masked(leaf_blocks, pattern)
    first = apply_rows(leaf_inverses[0, 0], leaf_rhs[0, 0])
    second = apply_rows(leaf_inverses[0, 1], leaf_rhs[0, 1] - apply_rows(blocks[0], first))
    upper_two = apply_rows(blocks[1], first) + apply_rows(blocks[2], second)
    upper_three = apply_rows(blocks[3], first) + apply_rows(blocks[4], second)
    upper_two, upper_three = lax.psum((upper_two, upper_three), "leaf")
    third = apply_rows(root_inverses[0], root_rhs[0] - upper_two)
    fourth = apply_rows(root_inverses[1], root_rhs[1] - upper_three - apply_rows(root_block, third))
    return (jnp.stack([first, second])[None], jnp.stack([third, fourth]))


def pairs(dest):
    out = []
    for r in range(2):
        for zh in range(2):
            for zl in range(2):
                for x in range(2):
                    for l in range(2):
                        d = dest(r, zh, zl, x, l)
                        if d is None:
                            continue
                        s = (r * 8 + zh * 4 + zl * 2 + x) * 2 + l
                        e = (d[0] * 8 + d[1] * 4 + d[2] * 2 + d[3]) * 2 + d[4]
                        out.append((s, e))
    return out


def send(value, dest):
    return lax.ppermute(value, AXES, pairs(dest))


def to_far(r, zh, zl, x, l):
    return r, zh ^ 1, zl, x, l


def to_second(r, zh, zl, x, l):
    return (r, zh, zl, x ^ 1, l) if l == 0 else (r ^ 1, zh, zl, x, l)


def to_third(r, zh, zl, x, l):
    return (r ^ 1, zh, zl, x, l) if l == 0 else (r, zh, zl, x ^ 1, l)


def to_pair(r, zh, zl, x, l):
    return r, zh, zl ^ 1, x, l


def to_core(r, zh, zl, x, l):
    return r, zh, zl, x, l ^ 1


def to_pair_core(r, zh, zl, x, l):
    return r, zh, zl ^ 1, x, l ^ 1


def to_far_pair(r, zh, zl, x, l):
    return r, zh ^ 1, zl ^ 1, x, l


def to_row(r, zh, zl, x, l):
    return r ^ 1, zh, zl, x, l


def to_group(b1, b2):
    return lambda r, zh, zl, x, l: (r, zh ^ b1, zl, x ^ b2, l)


def to_group_by_core(b1, b2):
    return lambda r, zh, zl, x, l: (r ^ l, zh ^ b1, zl, x ^ b2, l)


def after(value, *others):
    return lax.optimization_barrier((value,) + others)[0]


def vmem():
    return pl.BlockSpec(memory_space=pltpu.VMEM)


def smem():
    return pl.BlockSpec(memory_space=pltpu.SMEM)


def shaped(*dims):
    return jax.ShapeDtypeStruct(dims, F32)


def lanes_low():
    return lax.broadcasted_iota(jnp.int32, (1, 128), 1) < 64


def swap_lanes(one, two):
    low = lanes_low()
    even = jnp.where(low, one, pltpu.roll(two, 64, one.ndim - 1))
    odd = jnp.where(low, pltpu.roll(one, 64, one.ndim - 1), two)
    return even, odd


def split(value):
    high = value.astype(BF16)
    return high, (value - high.astype(F32)).astype(BF16)


def dot3(left, right):
    lh, ll = left
    rh, rl = right
    whole = jnp.dot(lh, rl, preferred_element_type=F32)
    whole += jnp.dot(ll, rh, preferred_element_type=F32)
    return whole + jnp.dot(lh, rh, preferred_element_type=F32)


def flat(value):
    return jnp.concatenate([value[:64], value[64:]], axis=1)


def spot():
    row, col, core = (lax.axis_index(name) for name in AXES)
    return row, col // 4, (col // 2) % 2, col % 2, core


def call(name, kernel, outs, *operands, specs=None, scratch=()):
    specs = specs or [None] * len(operands)
    fixed = [
        pltpu.with_memory_space_constraint(o, pltpu.VMEM) if s is None else o
        for o, s in zip(operands, specs)
    ]
    return pl.pallas_call(
        kernel,
        out_shape=[pltpu.VMEM(dims, F32) for dims in outs],
        in_specs=[vmem() if s is None else s for s in specs],
        out_specs=[vmem() for _ in outs],
        scratch_shapes=list(scratch),
        compiler_params=pltpu.CompilerParams(vmem_limit_bytes=VMEM_OF_A_KERNEL),
        name=name,
    )(*fixed)


def cut_columns(source, held, base):
    r = spot()[0]
    for p in range(2):
        for z in range(2):
            start = pl.multiple_of((2 * r + z) * 128, 128)
            one = source[p, 0, :, pl.ds(start, 128)]
            two = source[p, 1, :, pl.ds(start, 128)]
            even, odd = swap_lanes(one, two)
            held[2 * z, base + p] = even
            held[2 * z + 1, base + p] = odd


def part_rows(source, keep, out):
    zl = spot()[2]
    for a in range(2):
        even, odd = swap_lanes(source[a, :, :128], source[a, :, 128:])
        keep[a] = jnp.where(zl == 0, even, odd)
        out[a] = jnp.where(zl == 0, odd, even)


def begin_kernel(tiles, *refs):
    sources, outs, places = refs[:6], refs[6:16], refs[16:22]
    cuts, sems = refs[22:]
    copies = [
        pltpu.make_async_copy(source, place, sems.at[k])
        for k, (source, place) in enumerate(zip(sources, places))
    ]
    for copy in copies:
        copy.start()
    leaf_inv, blocks, leaf_rhs, root_rhs, root_inv, lower = places
    first_out, first, rest_out, rest, masked_out, lower_out = outs[:6]
    core = spot()[4]

    def mask(m, dest, base):
        for t in range(2):
            lanes = slice(t * 128, t * 128 + 128)
            weight = tiles[0, t, 0, m].astype(F32)
            for a in range(2):
                dest[base + t, a] = blocks[0, m, a, :, lanes] * weight

    copies[0].wait()
    part_rows(leaf_inv.at[0, 0], first.at[0], first_out)
    copies[1].wait()
    mask(0, first, 1)
    copies[2].wait()
    cut_columns(leaf_rhs.at[0], cuts, 0)
    copies[3].wait()
    cut_columns(root_rhs, cuts, 2)
    _, zh, _, x, _ = spot()
    for b1 in range(2):
        for b2 in range(2):
            outs[6 + b1 * 2 + b2][...] = cuts[(zh ^ b1) * 2 + (x ^ b2)]
    part_rows(leaf_inv.at[0, 1], rest.at[0], rest_out.at[0])
    copies[4].wait()
    part_rows(root_inv.at[core], rest.at[1], rest_out.at[1])
    copies[5].wait()
    for a in range(2):
        start = pl.multiple_of(core * 128, 128)
        lower_out[0, a] = lower[a, :, pl.ds(start, 128)]
    for m in range(1, 5):
        mask(m, masked_out, 2 * (m - 1))


def begin(pattern, *arrays):
    tiles = pattern.transpose(0, 2, 3, 1)
    units = [(2, 32, 128), (3, 2, 32, 128), (2, 2, 32, 128), (2, 2, 32, 128)]
    outs = units + [(8, 2, 32, 128), (1, 2, 32, 128)] + [(4, 32, 128)] * 4
    return pl.pallas_call(
        begin_kernel,
        out_shape=[pltpu.VMEM(dims, F32) for dims in outs],
        in_specs=[smem()] + [pl.BlockSpec(memory_space=pltpu.HBM)] * 6,
        out_specs=[vmem() for _ in outs],
        scratch_shapes=[pltpu.VMEM(a.shape, F32) for a in arrays]
        + [pltpu.VMEM((4, 4, 32, 128), F32), pltpu.SemaphoreType.DMA((6,))],
        compiler_params=pltpu.CompilerParams(vmem_limit_bytes=VMEM_OF_A_KERNEL),
        name="begin",
    )(tiles, *(pltpu.with_memory_space_constraint(a, pltpu.HBM) for a in arrays))


def fetch(pick, dest, sems, swapped=None, from_core=0):
    r, zh, _, x, l = spot()
    copies = []
    for b3 in range(2):
        for b2 in range(2):
            for b1 in range(2):

                def copy_of(source, core):
                    rr = r ^ jnp.where(core == 0, b3, b2)
                    xx = x ^ jnp.where(core == 0, b2, b3)
                    return pltpu.make_async_copy(
                        source(b3, b2, b1),
                        dest(rr, zh ^ b1, xx),
                        sems.at[b3 * 4 + b2 * 2 + b1],
                    )

                copy = copy_of(pick, l)
                if swapped is None:
                    copy.start()
                else:
                    pl.when(l == from_core)(copy.start)
                    pl.when(l != from_core)(copy_of(swapped, 1 - l).start)
                copies.append(copy)
    return copies


def wait_all(copies):
    for copy in copies:
        copy.wait()


def solve(inverse, vector):
    left = split(flat(vector))
    parts = [dot3(left, split(inverse[a].reshape(512, 128))) for a in range(2)]
    return jnp.concatenate(parts, axis=0)


def update(held, terms, waits):
    sums = [None, None]
    for t, vector in enumerate(terms):
        waits[t]()
        left = split(flat(vector))
        for a in range(2):
            right = jnp.concatenate(
                [held[t, a, 0].reshape(256, 128), held[t, a, 1].reshape(256, 128)], axis=1
            )
            part = dot3(left, split(right))
            sums[a] = part if sums[a] is None else sums[a] + part
    return jnp.concatenate(sums, axis=0)


def sum_four(refs):
    return (refs[0][...] + refs[1][...]) + (refs[2][...] + refs[3][...])


def inverse_place(inverse):
    return lambda r, zh, x: inverse.at[r, :, zh, :, x]


def block_place(held, t):
    return lambda r, zh, x: held.at[t, r, :, :, zh, x]


def half_place(held, t, half):
    return lambda r, zh, x: held.at[t, r, half, :, zh, x]


def whole_chunk(four, third, m):
    return lambda b3, b2, b1: (four, third)[b3].at[b2 * 2 + b1, m]


def two_chunks(near, far, start, far_start):
    def pick(b3, b2, b1):
        ref = (near, far)[b1][b3]
        return ref.at[b2, pl.ds((start, far_start)[b1], 2)]

    return pick


def root_chunk(near, far, start, count):
    if count == 2:
        return lambda b3, b2, b1: (near, far)[b1].at[b3 * 2 + b2, pl.ds(start, 2)]
    return lambda b3, b2, b1: (near, far)[b1].at[b3 * 2 + b2, start]


def link_0_kernel(b_ref, four, third, part_ref, y_ref, inverse, held, sems):
    first = fetch(whole_chunk(four, third, 0), inverse_place(inverse), sems.at[0])
    second = fetch(whole_chunk(four, third, 1), block_place(held, 0), sems.at[1])
    wait_all(first)
    solved = solve(inverse, b_ref[...])
    y_ref[...] = solved
    part_ref[...] = update(held, [solved], [functools.partial(wait_all, second)])


def link_1_kernel(b_ref, own, got, y0_ref, n0, n1, f0, f1, part_ref, y_ref, inverse, held, sems):
    near, far = (n0, n1), (f0, f1)
    copies = [fetch(two_chunks(near, far, 0, 0), inverse_place(inverse), sems.at[0])]
    for t in range(2):
        pick = two_chunks(near, far, 2 * t + 2, 2 * t + 2)
        copies.append(fetch(pick, block_place(held, t), sems.at[t + 1]))
    wait_all(copies[0])
    solved = solve(inverse, b_ref[...] - (own[...] + got[...]))
    y_ref[...] = solved
    waits = [functools.partial(wait_all, c) for c in copies[1:]]
    part_ref[...] = update(held, [y0_ref[...], solved], waits)


def link_2_kernel(b_ref, s0, s1, s2, s3, y0_ref, y1_ref, n0, n1, f0, f1, *refs):
    near, far = (n0, n1), (f0, f1)
    root, swapped = refs[:2], refs[2:4]
    part_ref, y_ref, inverse, held, sems = refs[4:]
    first = fetch(
        root_chunk(*root, 0, 2), inverse_place(inverse), sems.at[0], root_chunk(*swapped, 0, 2), 0
    )
    copies = [
        fetch(two_chunks(near, far, 9 + 2 * t, 2 * t), block_place(held, t), sems.at[t + 1])
        for t in range(2)
    ]
    halves = [
        fetch(
            root_chunk(*root, 2, 1), half_place(held, 2, h), sems.at[3 + h], root_chunk(*swapped, 2, 1), h
        )
        for h in range(2)
    ]
    wait_all(first)
    solved = solve(inverse, b_ref[...] - sum_four((s0, s1, s2, s3)))
    y_ref[...] = solved
    copies.append(halves[0] + halves[1])
    waits = [functools.partial(wait_all, c) for c in copies]
    last = jnp.where(spot()[4] == 0, solved, 0.0)
    part_ref[...] = update(held, [y0_ref[...], y1_ref[...], last], waits)


def link_3_kernel(b_ref, s0, s1, s2, s3, y2_ref, *refs):
    root, swapped, outs = refs[:2], refs[2:4], refs[4:8]
    pieces, inverse, sems = refs[8:]
    first = fetch(
        root_chunk(*root, 0, 2), inverse_place(inverse), sems.at[0], root_chunk(*swapped, 0, 2), 1
    )
    vector = b_ref[...] - sum_four((s0, s1, s2, s3))
    wait_all(first)
    lay_values((y2_ref[...], solve(inverse, vector)), outs, pieces)


def link_scratch(nblocks, nsems):
    blocks = [pltpu.VMEM((nblocks, 2, 2, 2, 2, 2, 32, 128), F32)] if nblocks else []
    return (
        [pltpu.VMEM((2, 2, 2, 2, 2, 32, 128), F32)] + blocks + [pltpu.SemaphoreType.DMA((nsems, 8))]
    )


def lay_values(values, outs, held):
    _, zh, _, x, _ = spot()
    for p, value in enumerate(values):
        held[:, p] = value.T.reshape(4, 32, 128)
    for b1 in range(2):
        for b2 in range(2):
            outs[b1 * 2 + b2][...] = held[(zh ^ b1) * 2 + (x ^ b2)]


def lay_kernel(first, second, *refs):
    lay_values((first[...], second[...]), refs[:4], refs[4])


def stand_kernel(near_ref, other_ref, *refs):
    outs, held = refs[:4], refs[4]
    _, zh, zl, x, _ = spot()
    for b1 in range(2):
        for b2 in range(2):
            for b, source in enumerate((near_ref, other_ref)):
                held[((zh ^ b1) * 2 + (zl ^ b)) * 2 + (x ^ b2)] = source[b1 * 2 + b2]
    for p, out in enumerate(outs):
        out[...] = held[:, p].reshape(256, 128).T


def join_kernel(by_core, near_ref, other_ref, out_ref, held):
    r, zh, _, x, core = spot()
    near = r ^ core if by_core else r
    for b1 in range(2):
        for b2 in range(2):
            place = (zh ^ b1) * 2 + (x ^ b2)
            held[near * 4 + place] = near_ref[b1 * 2 + b2]
            held[(near ^ 1) * 4 + place] = other_ref[b1 * 2 + b2]
    for p in range(2):
        for u in range(4):
            lanes = slice(u * 128, u * 128 + 128)
            out_ref[p, 0, :, lanes], out_ref[p, 1, :, lanes] = swap_lanes(
                held[2 * u, p], held[2 * u + 1, p]
            )


def join(name, by_core, near, other):
    return pl.pallas_call(
        functools.partial(join_kernel, by_core),
        out_shape=shaped(2, 2, 32, 512),
        in_specs=[vmem()] * 2,
        out_specs=vmem(),
        scratch_shapes=[pltpu.VMEM((8, 2, 32, 128), F32)],
        compiler_params=pltpu.CompilerParams(vmem_limit_bytes=VMEM_OF_A_KERNEL),
        name=name,
    )(*(pltpu.with_memory_space_constraint(v, pltpu.VMEM) for v in (near, other)))


def to_groups(parts):
    return [parts[0]] + [send(parts[k], to_group(k // 2, k % 2)) for k in (1, 2, 3)]


PIECES = [(2, 32, 128)] * 4
VECTOR = [(128, 256), (128, 128)]


def grouped(leaf_rhs, root_rhs, leaf_inverses, root_inverses, leaf_blocks, root_block, pattern):
    zl = (lax.axis_index("col") // 2) % 2
    four_pieces = pltpu.VMEM((4, 2, 32, 128), F32)

    def whole(keep, got):
        return jnp.stack([jnp.where(zl == 0, keep, got), jnp.where(zl == 0, got, keep)], axis=-3)

    first_out, first, rest_out, rest, blocks, lower, *cuts = begin(
        pattern, leaf_inverses, leaf_blocks, leaf_rhs, root_rhs, root_inverses, root_block
    )
    first_pair = send(first_out, to_pair)
    first_far = send(first, to_far)
    first_far_pair = send(first_out, to_far_pair)
    rest_pair = send(rest_out, to_pair)
    moved = to_groups(cuts)

    inverses = whole(rest, rest_pair)
    own_units = jnp.concatenate([inverses[0], blocks[:4], inverses[1], lower, blocks[4:]])
    second_own = send(own_units, to_second)

    def first_chunk(values, got):
        return jnp.stack([whole(values[0], got), values[1:]])

    two_a = jnp.stack(
        [
            first_chunk(first, first_pair),
            first_chunk(after(first_far, own_units), first_far_pair),
        ]
    )
    second_a = send(two_a, to_second)
    far_b = send(after(own_units[:9], two_a), to_far)
    rhs_in = jnp.stack(after(moved, two_a))
    rhs_pair = send(rhs_in, to_pair)
    near_0 = jnp.stack([own_units, after(second_own, rhs_in)])
    near_1 = send(near_0, to_third)
    four_a = jnp.concatenate([two_a, after(second_a, near_0)])
    third_a = send(four_a, to_third)
    b0, b1, r2, r3 = call(
        "stand",
        stand_kernel,
        [(128, 256)] * 4,
        after(rhs_in, four_a),
        rhs_pair,
        scratch=[pltpu.VMEM((8, 4, 32, 128), F32)],
    )
    far_b = after(far_b, b0)
    second_b = send(far_b, to_second)
    far_c = send(after(own_units[9:], far_b), to_far)
    far_b_0 = jnp.stack([far_b, second_b])
    far_b_1 = send(far_b_0, to_third)

    own, y0 = call(
        "link_0",
        link_0_kernel,
        VECTOR,
        after(b0, far_b),
        four_a,
        third_a,
        scratch=link_scratch(1, 2),
    )
    got = send(own, to_pair)
    far_c = after(far_c, got)
    second_c = send(far_c, to_second)
    root_near = jnp.concatenate([near_0[:, 6:9], after(near_1, got)[:, 6:9]])
    swap_near = send(root_near, to_core)

    own, y1 = call(
        "link_1",
        link_1_kernel,
        VECTOR,
        after(b1, far_c),
        own,
        got,
        y0,
        near_0,
        near_1,
        far_b_0,
        far_b_1,
        scratch=link_scratch(2, 3),
    )
    sums = [own, send(own, to_pair), send(own, to_core), send(own, to_pair_core)]
    root_far = jnp.concatenate([far_b_0[:, 6:9], after(far_b_1, own)[:, 6:9]])
    swap_far = send(root_far, to_core)
    far_c_0 = jnp.stack([far_c, after(second_c, own)])
    far_c_1 = send(far_c_0, to_third)
    leaf_parts = call("lay_leaf", lay_kernel, PIECES, after(y0, far_c_0), y1, scratch=[four_pieces])
    leaf_moved = to_groups(leaf_parts)

    own, y2 = call(
        "link_2",
        link_2_kernel,
        VECTOR,
        after(r2, leaf_parts[0]),
        *sums,
        y0,
        y1,
        near_0,
        near_1,
        far_c_0,
        far_c_1,
        root_near,
        root_far,
        swap_near,
        swap_far,
        scratch=link_scratch(3, 5),
    )
    sums = [own, send(own, to_pair), send(own, to_core), send(own, to_pair_core)]
    leaf_near = jnp.stack(after(leaf_moved, own))
    leaf_other = send(leaf_near, to_row)
    leaf_solution = join("join_leaf", False, leaf_near, leaf_other)

    root_parts = call(
        "link_3",
        link_3_kernel,
        PIECES,
        after(r3, leaf_near),
        *sums,
        y2,
        root_near,
        root_far,
        swap_near,
        swap_far,
        scratch=[four_pieces] + link_scratch(0, 1),
    )
    moved = jnp.stack([send(root_parts[k], to_group_by_core(k // 2, k % 2)) for k in range(4)])
    swapped = send(moved, to_core)
    root_solution = join("join_root", True, moved, swapped)
    return leaf_solution[None], root_solution


def solution(mesh):
    placed = (
        P("leaf", None, None, "col", None),
        P(None, None, "col", None),
        P("leaf", None, None, "col", "row"),
        P(None, None, "col", "row"),
        P("leaf", None, None, "col", "row"),
        P(None, "col", "row"),
        P("leaf", None, "row", "col"),
    )
    small = (mesh.shape["row"], mesh.shape["col"], mesh.shape["leaf"]) == (2, 8, 2)
    return jax.shard_map(
        grouped if small else general,
        mesh=mesh,
        in_specs=placed,
        out_specs=(P("leaf", None, None, "col", None), P(None, None, "col", None)),
        check_vma=False,
    )
```

```python
import functools

import jax
import jax.numpy as jnp
from jax import lax
from jax.experimental import pallas as pl
from jax.experimental.pallas import tpu as pltpu
from jax.sharding import PartitionSpec as P

BLK = 128
AXES = ("row", "col", "leaf")
F32 = jnp.float32
BF16 = jnp.bfloat16
VMEM_OF_A_KERNEL = 16 * 2**20


def apply_rows(block, vector):
    block = block.reshape(-1, block.shape[-1])
    vector = vector.reshape(-1, vector.shape[-1])
    term = lax.dot_general(
        block,
        vector,
        (((0,), (0,)), ((), ())),
        precision=lax.Precision.HIGHEST,
        preferred_element_type=F32,
    )
    owned = lax.psum_scatter(term, "col", scatter_dimension=0, tiled=True)
    return lax.all_gather(owned[None], "row", axis=0, tiled=True)


def masked(leaf_blocks, pattern):
    local = leaf_blocks[0]
    shaped = local.reshape(local.shape[:3] + (local.shape[3] // BLK, BLK))
    weights = pattern[0].astype(F32).transpose(0, 2, 1)[:, None, :, :, None]
    return (shaped * weights).reshape(local.shape)


def general(leaf_rhs, root_rhs, leaf_inverses, root_inverses, leaf_blocks, root_block, pattern):
    blocks = masked(leaf_blocks, pattern)
    first = apply_rows(leaf_inverses[0, 0], leaf_rhs[0, 0])
    second = apply_rows(leaf_inverses[0, 1], leaf_rhs[0, 1] - apply_rows(blocks[0], first))
    upper_two = apply_rows(blocks[1], first) + apply_rows(blocks[2], second)
    upper_three = apply_rows(blocks[3], first) + apply_rows(blocks[4], second)
    upper_two, upper_three = lax.psum((upper_two, upper_three), "leaf")
    third = apply_rows(root_inverses[0], root_rhs[0] - upper_two)
    fourth = apply_rows(root_inverses[1], root_rhs[1] - upper_three - apply_rows(root_block, third))
    return (jnp.stack([first, second])[None], jnp.stack([third, fourth]))


def pairs(dest):
    out = []
    for r in range(2):
        for zh in range(2):
            for zl in range(2):
                for x in range(2):
                    for l in range(2):
                        d = dest(r, zh, zl, x, l)
                        if d is None:
                            continue
                        s = (r * 8 + zh * 4 + zl * 2 + x) * 2 + l
                        e = (d[0] * 8 + d[1] * 4 + d[2] * 2 + d[3]) * 2 + d[4]
                        out.append((s, e))
    return out


def send(value, dest):
    return lax.ppermute(value, AXES, pairs(dest))


def to_far(r, zh, zl, x, l):
    return r, zh ^ 1, zl, x, l


def to_second(r, zh, zl, x, l):
    return (r, zh, zl, x ^ 1, l) if l == 0 else (r ^ 1, zh, zl, x, l)


def to_third(r, zh, zl, x, l):
    return (r ^ 1, zh, zl, x, l) if l == 0 else (r, zh, zl, x ^ 1, l)


def to_pair(r, zh, zl, x, l):
    return r, zh, zl ^ 1, x, l


def to_core(r, zh, zl, x, l):
    return r, zh, zl, x, l ^ 1


def to_pair_core(r, zh, zl, x, l):
    return r, zh, zl ^ 1, x, l ^ 1


def to_far_pair(r, zh, zl, x, l):
    return r, zh ^ 1, zl ^ 1, x, l


def to_row(r, zh, zl, x, l):
    return r ^ 1, zh, zl, x, l


def to_group(b1, b2):
    return lambda r, zh, zl, x, l: (r, zh ^ b1, zl, x ^ b2, l)


def to_group_by_core(b1, b2):
    return lambda r, zh, zl, x, l: (r ^ l, zh ^ b1, zl, x ^ b2, l)


def after(value, *others):
    return lax.optimization_barrier((value,) + others)[0]


def vmem():
    return pl.BlockSpec(memory_space=pltpu.VMEM)


def smem():
    return pl.BlockSpec(memory_space=pltpu.SMEM)


def shaped(*dims):
    return jax.ShapeDtypeStruct(dims, F32)


def lanes_low():
    return lax.broadcasted_iota(jnp.int32, (1, 128), 1) < 64


def swap_lanes(one, two):
    low = lanes_low()
    even = jnp.where(low, one, pltpu.roll(two, 64, one.ndim - 1))
    odd = jnp.where(low, pltpu.roll(one, 64, one.ndim - 1), two)
    return even, odd


def split(value):
    high = value.astype(BF16)
    return high, (value - high.astype(F32)).astype(BF16)


def dot3(left, right):
    lh, ll = left
    rh, rl = right
    whole = jnp.dot(lh, rl, preferred_element_type=F32)
    whole += jnp.dot(ll, rh, preferred_element_type=F32)
    return whole + jnp.dot(lh, rh, preferred_element_type=F32)


def flat(value):
    return jnp.concatenate([value[:64], value[64:]], axis=1)


def spot():
    row, col, core = (lax.axis_index(name) for name in AXES)
    return row, col // 4, (col // 2) % 2, col % 2, core


def call(name, kernel, outs, *operands, specs=None, scratch=()):
    specs = specs or [None] * len(operands)
    fixed = [
        pltpu.with_memory_space_constraint(o, pltpu.VMEM) if s is None else o
        for o, s in zip(operands, specs)
    ]
    return pl.pallas_call(
        kernel,
        out_shape=[pltpu.VMEM(dims, F32) for dims in outs],
        in_specs=[vmem() if s is None else s for s in specs],
        out_specs=[vmem() for _ in outs],
        scratch_shapes=list(scratch),
        compiler_params=pltpu.CompilerParams(vmem_limit_bytes=VMEM_OF_A_KERNEL),
        name=name,
    )(*fixed)


def cut_columns(source, held, base):
    r = spot()[0]
    for p in range(2):
        for z in range(2):
            start = pl.multiple_of((2 * r + z) * 128, 128)
            one = source[p, 0, :, pl.ds(start, 128)]
            two = source[p, 1, :, pl.ds(start, 128)]
            even, odd = swap_lanes(one, two)
            held[2 * z, base + p] = even
            held[2 * z + 1, base + p] = odd


def part_rows(source, keep, out):
    zl = spot()[2]
    for a in range(2):
        even, odd = swap_lanes(source[a, :, :128], source[a, :, 128:])
        keep[a] = jnp.where(zl == 0, even, odd)
        out[a] = jnp.where(zl == 0, odd, even)


def begin_kernel(tiles, *refs):
    sources, outs, places = refs[:6], refs[6:15], refs[15:21]
    cuts, sems = refs[21:]
    copies = [
        pltpu.make_async_copy(source, place, sems.at[k])
        for k, (source, place) in enumerate(zip(sources, places))
    ]
    for copy in copies:
        copy.start()
    leaf_inv, blocks, leaf_rhs, root_rhs, root_inv, lower = places
    away, first, rest, masked_out, lower_out = outs[:5]
    core = spot()[4]

    def mask(m, dest, base):
        for t in range(2):
            lanes = slice(t * 128, t * 128 + 128)
            weight = tiles[0, t, 0, m].astype(F32)
            for a in range(2):
                dest[base + t, a] = blocks[0, m, a, :, lanes] * weight

    copies[0].wait()
    part_rows(leaf_inv.at[0, 0], first.at[0], away.at[0])
    copies[1].wait()
    mask(0, first, 1)
    copies[2].wait()
    cut_columns(leaf_rhs.at[0], cuts, 0)
    copies[3].wait()
    cut_columns(root_rhs, cuts, 2)
    _, zh, _, x, _ = spot()
    for b1 in range(2):
        for b2 in range(2):
            outs[5 + b1 * 2 + b2][...] = cuts[(zh ^ b1) * 2 + (x ^ b2)]
    part_rows(leaf_inv.at[0, 1], rest.at[0], away.at[1])
    copies[4].wait()
    part_rows(root_inv.at[core], rest.at[1], away.at[2])
    copies[5].wait()
    for a in range(2):
        start = pl.multiple_of(core * 128, 128)
        lower_out[0, a] = lower[a, :, pl.ds(start, 128)]
    for m in range(1, 5):
        mask(m, masked_out, 2 * (m - 1))


def begin(pattern, *arrays):
    tiles = pattern.transpose(0, 2, 3, 1)
    outs = [(3, 2, 32, 128), (3, 2, 32, 128), (2, 2, 32, 128)] + [(8, 2, 32, 128), (1, 2, 32, 128)] + [(4, 32, 128)] * 4
    return pl.pallas_call(
        begin_kernel,
        out_shape=[pltpu.VMEM(dims, F32) for dims in outs],
        in_specs=[smem()] + [pl.BlockSpec(memory_space=pltpu.HBM)] * 6,
        out_specs=[vmem() for _ in outs],
        scratch_shapes=[pltpu.VMEM(a.shape, F32) for a in arrays]
        + [pltpu.VMEM((4, 4, 32, 128), F32), pltpu.SemaphoreType.DMA((6,))],
        compiler_params=pltpu.CompilerParams(vmem_limit_bytes=VMEM_OF_A_KERNEL),
        name="begin",
    )(tiles, *(pltpu.with_memory_space_constraint(a, pltpu.HBM) for a in arrays))


def fetch(pick, dest, sems, swapped=None, from_core=0):
    r, zh, _, x, l = spot()
    copies = []
    for b3 in range(2):
        for b2 in range(2):
            for b1 in range(2):

                def copy_of(source, core):
                    rr = r ^ jnp.where(core == 0, b3, b2)
                    xx = x ^ jnp.where(core == 0, b2, b3)
                    return pltpu.make_async_copy(
                        source(b3, b2, b1),
                        dest(rr, zh ^ b1, xx),
                        sems.at[b3 * 4 + b2 * 2 + b1],
                    )

                copy = copy_of(pick, l)
                if swapped is None:
                    copy.start()
                else:
                    pl.when(l == from_core)(copy.start)
                    pl.when(l != from_core)(copy_of(swapped, 1 - l).start)
                copies.append(copy)
    return copies


def wait_all(copies):
    for copy in copies:
        copy.wait()


def solve(inverse, vector):
    left = split(flat(vector))
    parts = [dot3(left, split(inverse[a].reshape(512, 128))) for a in range(2)]
    return jnp.concatenate(parts, axis=0)


def update(held, terms, waits):
    sums = [None, None]
    for t, vector in enumerate(terms):
        waits[t]()
        left = split(flat(vector))
        for a in range(2):
            right = jnp.concatenate(
                [held[t, a, 0].reshape(256, 128), held[t, a, 1].reshape(256, 128)], axis=1
            )
            part = dot3(left, split(right))
            sums[a] = part if sums[a] is None else sums[a] + part
    return jnp.concatenate(sums, axis=0)


def sum_four(refs):
    return (refs[0][...] + refs[2][...]) + (refs[1][...] + refs[3][...])


def first_chunk_unit(four, third):
    return lambda unit: lambda b3, b2, b1: (four, third)[b3].at[b2 * 2 + b1, unit]


def chunk_unit(near, far, start, far_start):
    def of(unit):
        def pick(b3, b2, b1):
            return (near, far)[b1][b3].at[b2, (start, far_start)[b1] + unit]

        return pick

    return of


def root_unit(ref):
    return lambda unit: lambda b3, b2, b1: ref.at[b1 * 4 + b3 * 2 + b2, unit]


def fetch_inverse(unit, inverse, sems, swapped=None, from_core=0):
    copies = []
    for half in range(2):
        copies += fetch(
            unit(half),
            lambda r, zh, x, half=half: inverse.at[r, :, zh, half, x],
            sems.at[half],
            swapped and swapped(half),
            from_core,
        )
    return copies


def fetch_block(unit, held, t, sems):
    copies = []
    for half in range(2):
        copies += fetch(
            unit(half), lambda r, zh, x, half=half: held.at[t, r, half, :, zh, x], sems.at[half]
        )
    return copies


def fetch_halves(root, swapped, held, t, sems):
    copies = []
    for half in range(2):
        copies += fetch(
            root(2),
            lambda r, zh, x, half=half: held.at[t, r, half, :, zh, x],
            sems.at[half],
            swapped(2),
            half,
        )
    return copies


def shifted(unit, by):
    return lambda half: unit(half + by)


def link_0_kernel(b_ref, four, third, part_ref, y_ref, inverse, held, sems):
    unit = first_chunk_unit(four, third)
    first = fetch_inverse(unit, inverse, sems.at[0])
    second = fetch_block(shifted(unit, 2), held, 0, sems.at[1])
    wait_all(first)
    solved = solve(inverse, b_ref[...])
    y_ref[...] = solved
    part_ref[...] = update(held, [solved], [functools.partial(wait_all, second)])


def link_1_kernel(b_ref, own, got, y0_ref, n0, n1, f0, f1, part_ref, y_ref, inverse, held, sems):
    unit = chunk_unit((n0, n1), (f0, f1), 0, 0)
    first = fetch_inverse(unit, inverse, sems.at[0])
    copies = [fetch_block(shifted(unit, 2 * t + 2), held, t, sems.at[t + 1]) for t in range(2)]
    wait_all(first)
    solved = solve(inverse, b_ref[...] - (own[...] + got[...]))
    y_ref[...] = solved
    waits = [functools.partial(wait_all, c) for c in copies]
    part_ref[...] = update(held, [y0_ref[...], solved], waits)


def link_2_kernel(b_ref, s0, s1, s2, s3, y0_ref, y1_ref, n0, n1, f0, f1, root, swapped, *refs):
    part_ref, y_ref, inverse, held, sems = refs
    unit = chunk_unit((n0, n1), (f0, f1), 9, 0)
    root, swapped = root_unit(root), root_unit(swapped)
    first = fetch_inverse(root, inverse, sems.at[0], swapped, 0)
    copies = [fetch_block(shifted(unit, 2 * t), held, t, sems.at[t + 1]) for t in range(2)]
    copies.append(fetch_halves(root, swapped, held, 2, sems.at[3]))
    wait_all(first)
    solved = solve(inverse, b_ref[...] - sum_four((s0, s1, s2, s3)))
    y_ref[...] = solved
    waits = [functools.partial(wait_all, c) for c in copies]
    last = jnp.where(spot()[4] == 0, solved, 0.0)
    part_ref[...] = update(held, [y0_ref[...], y1_ref[...], last], waits)


def link_3_kernel(b_ref, s0, s1, s2, s3, y0_ref, y1_ref, y2_ref, root, swapped, *refs):
    outs, (pieces, inverse, sems) = refs[:4], refs[4:]
    first = fetch_inverse(root_unit(root), inverse, sems.at[0], root_unit(swapped), 1)
    vector = b_ref[...] - sum_four((s0, s1, s2, s3))
    lay_values((y0_ref, y1_ref, y2_ref), pieces)
    wait_all(first)
    pieces[:, 3] = solve(inverse, vector).T.reshape(4, 32, 128)
    _, zh, _, x, _ = spot()
    for b1 in range(2):
        for b2 in range(2):
            outs[b1 * 2 + b2][...] = pieces[(zh ^ b1) * 2 + (x ^ b2)]


def link_scratch(nblocks, nsems):
    blocks = [pltpu.VMEM((nblocks, 2, 2, 2, 2, 2, 32, 128), F32)] if nblocks else []
    return (
        [pltpu.VMEM((2, 2, 2, 2, 2, 32, 128), F32)] + blocks + [pltpu.SemaphoreType.DMA((nsems, 2, 8))]
    )


def lay_values(refs, held):
    for p, ref in enumerate(refs):
        held[:, p] = ref[...].T.reshape(4, 32, 128)


def stand_kernel(near_ref, other_ref, *refs):
    outs, held = refs[:4], refs[4]
    _, zh, zl, x, _ = spot()
    for b1 in range(2):
        for b2 in range(2):
            for b, source in enumerate((near_ref, other_ref)):
                held[((zh ^ b1) * 2 + (zl ^ b)) * 2 + (x ^ b2)] = source[b1 * 2 + b2]
    for p, out in enumerate(outs):
        out[...] = held[:, p].reshape(256, 128).T


def join_kernel(near_ref, other_ref, out_ref, held):
    r, zh, _, x, core = spot()
    near = r ^ core
    for b1 in range(2):
        for b2 in range(2):
            place = (zh ^ b1) * 2 + (x ^ b2)
            held[near * 4 + place] = near_ref[b1 * 2 + b2]
            held[(near ^ 1) * 4 + place] = other_ref[b1 * 2 + b2]
    for p in range(2):
        for u in range(4):
            lanes = slice(u * 128, u * 128 + 128)
            out_ref[p, 0, :, lanes], out_ref[p, 1, :, lanes] = swap_lanes(
                held[2 * u, p], held[2 * u + 1, p]
            )


def join(name, near, other):
    return pl.pallas_call(
        join_kernel,
        out_shape=shaped(2, 2, 32, 512),
        in_specs=[vmem()] * 2,
        out_specs=vmem(),
        scratch_shapes=[pltpu.VMEM((8, 2, 32, 128), F32)],
        compiler_params=pltpu.CompilerParams(vmem_limit_bytes=VMEM_OF_A_KERNEL),
        name=name,
    )(*(pltpu.with_memory_space_constraint(v, pltpu.VMEM) for v in (near, other)))


def to_groups(parts):
    return [parts[0]] + [send(parts[k], to_group(k // 2, k % 2)) for k in (1, 2, 3)]


VECTOR = [(128, 256), (128, 128)]


def grouped(leaf_rhs, root_rhs, leaf_inverses, root_inverses, leaf_blocks, root_block, pattern):
    zl = (lax.axis_index("col") // 2) % 2

    def whole(keep, got):
        return jnp.stack([jnp.where(zl == 0, keep, got), jnp.where(zl == 0, got, keep)])

    away, first, rest, blocks, lower, *cuts = begin(
        pattern, leaf_inverses, leaf_blocks, leaf_rhs, root_rhs, root_inverses, root_block
    )
    pair = send(away, to_pair)
    first_far = send(first, to_far)
    first_far_pair = send(away[0], to_far_pair)

    def first_chunk(values, got):
        return jnp.concatenate([whole(values[0], got), values[1:]])

    two_a = jnp.stack([first_chunk(first, pair[0]), first_chunk(first_far, first_far_pair)])
    second_a = send(two_a, to_second)

    late = after(pair, two_a)
    own_units = jnp.concatenate(
        [whole(rest[0], late[1]), blocks[:4], whole(rest[1], late[2]), lower, blocks[4:]]
    )
    far_b = send(own_units[:9], to_far)
    second_own = send(own_units, to_second)
    moved = to_groups(after(cuts, two_a))
    rhs_in = jnp.stack(moved)
    rhs_pair = send(rhs_in, to_pair)
    four_a = jnp.concatenate([two_a, second_a])
    third_a = send(four_a, to_third)
    near_0 = jnp.stack([own_units, after(second_own, third_a)])
    near_1 = send(near_0, to_third)
    far_b = after(far_b, third_a)
    second_b = send(far_b, to_second)
    far_c = send(after(own_units[9:], far_b), to_far)
    b0, b1, r2, r3 = call(
        "stand",
        stand_kernel,
        [(128, 256)] * 4,
        after(rhs_in, third_a),
        rhs_pair,
        scratch=[pltpu.VMEM((8, 4, 32, 128), F32)],
    )

    own, y0 = call(
        "link_0",
        link_0_kernel,
        VECTOR,
        after(b0, near_0, far_b),
        four_a,
        third_a,
        scratch=link_scratch(1, 2),
    )
    got = send(own, to_pair)
    far_b_0 = jnp.stack([far_b, after(second_b, got)])
    far_b_1 = send(far_b_0, to_third)
    far_c = after(far_c, got)
    second_c = send(far_c, to_second)

    own, y1 = call(
        "link_1",
        link_1_kernel,
        VECTOR,
        after(b1, far_c),
        own,
        got,
        y0,
        near_0,
        near_1,
        far_b_0,
        far_b_1,
        scratch=link_scratch(2, 3),
    )
    sums = [own, send(own, to_core), send(own, to_pair), send(own, to_pair_core)]
    root_own = jnp.concatenate(
        [after(near_0[:, 6:9], own), near_1[:, 6:9], far_b_0[:, 6:9], far_b_1[:, 6:9]]
    )
    root_swapped = send(root_own, to_core)
    far_c_0 = jnp.stack([far_c, after(second_c, own)])
    far_c_1 = send(far_c_0, to_third)

    own, y2 = call(
        "link_2",
        link_2_kernel,
        VECTOR,
        r2,
        *sums,
        y0,
        y1,
        near_0,
        near_1,
        far_c_0,
        far_c_1,
        root_own,
        root_swapped,
        scratch=link_scratch(3, 4),
    )
    sums = [own, send(own, to_core), send(own, to_pair), send(own, to_pair_core)]
    parts = call(
        "link_3",
        link_3_kernel,
        [(4, 32, 128)] * 4,
        r3,
        *sums,
        y0,
        y1,
        y2,
        root_own,
        root_swapped,
        scratch=[pltpu.VMEM((4, 4, 32, 128), F32)] + link_scratch(0, 1),
    )
    moved = jnp.stack([send(parts[k], to_group_by_core(k // 2, k % 2)) for k in range(4)])
    leaf_near, root_near = moved[:, :2], moved[:, 2:]
    leaf_other = send(leaf_near, to_row)
    root_other = send(root_near, to_core)
    return (
        join("join_leaf", leaf_near, leaf_other)[None],
        join("join_root", root_near, root_other),
    )


def solution(mesh):
    placed = (
        P("leaf", None, None, "col", None),
        P(None, None, "col", None),
        P("leaf", None, None, "col", "row"),
        P(None, None, "col", "row"),
        P("leaf", None, None, "col", "row"),
        P(None, "col", "row"),
        P("leaf", None, "row", "col"),
    )
    small = (mesh.shape["row"], mesh.shape["col"], mesh.shape["leaf"]) == (2, 8, 2)
    return jax.shard_map(
        grouped if small else general,
        mesh=mesh,
        in_specs=placed,
        out_specs=(P("leaf", None, None, "col", None), P(None, None, "col", None)),
        check_vma=False,
    )
```

```python
import functools

import jax
import jax.numpy as jnp
from jax import lax
from jax.experimental import pallas as pl
from jax.experimental.pallas import tpu as pltpu
from jax.sharding import PartitionSpec as P

BLK = 128
AXES = ("row", "col", "leaf")
F32 = jnp.float32
BF16 = jnp.bfloat16
VMEM_OF_A_KERNEL = 16 * 2**20


def apply_rows(block, vector):
    block = block.reshape(-1, block.shape[-1])
    vector = vector.reshape(-1, vector.shape[-1])
    term = lax.dot_general(
        block,
        vector,
        (((0,), (0,)), ((), ())),
        precision=lax.Precision.HIGHEST,
        preferred_element_type=F32,
    )
    owned = lax.psum_scatter(term, "col", scatter_dimension=0, tiled=True)
    return lax.all_gather(owned[None], "row", axis=0, tiled=True)


def masked(leaf_blocks, pattern):
    local = leaf_blocks[0]
    shaped = local.reshape(local.shape[:3] + (local.shape[3] // BLK, BLK))
    weights = pattern[0].astype(F32).transpose(0, 2, 1)[:, None, :, :, None]
    return (shaped * weights).reshape(local.shape)


def general(leaf_rhs, root_rhs, leaf_inverses, root_inverses, leaf_blocks, root_block, pattern):
    blocks = masked(leaf_blocks, pattern)
    first = apply_rows(leaf_inverses[0, 0], leaf_rhs[0, 0])
    second = apply_rows(leaf_inverses[0, 1], leaf_rhs[0, 1] - apply_rows(blocks[0], first))
    upper_two = apply_rows(blocks[1], first) + apply_rows(blocks[2], second)
    upper_three = apply_rows(blocks[3], first) + apply_rows(blocks[4], second)
    upper_two, upper_three = lax.psum((upper_two, upper_three), "leaf")
    third = apply_rows(root_inverses[0], root_rhs[0] - upper_two)
    fourth = apply_rows(root_inverses[1], root_rhs[1] - upper_three - apply_rows(root_block, third))
    return (jnp.stack([first, second])[None], jnp.stack([third, fourth]))


def pairs(dest):
    out = []
    for r in range(2):
        for zh in range(2):
            for zl in range(2):
                for x in range(2):
                    for l in range(2):
                        d = dest(r, zh, zl, x, l)
                        if d is None:
                            continue
                        s = (r * 8 + zh * 4 + zl * 2 + x) * 2 + l
                        e = (d[0] * 8 + d[1] * 4 + d[2] * 2 + d[3]) * 2 + d[4]
                        out.append((s, e))
    return out


def send(value, dest):
    return lax.ppermute(value, AXES, pairs(dest))


def to_far(r, zh, zl, x, l):
    return r, zh ^ 1, zl, x, l


def to_second(r, zh, zl, x, l):
    return (r, zh, zl, x ^ 1, l) if l == 0 else (r ^ 1, zh, zl, x, l)


def to_third(r, zh, zl, x, l):
    return (r ^ 1, zh, zl, x, l) if l == 0 else (r, zh, zl, x ^ 1, l)


def to_pair(r, zh, zl, x, l):
    return r, zh, zl ^ 1, x, l


def to_core(r, zh, zl, x, l):
    return r, zh, zl, x, l ^ 1


def to_pair_core(r, zh, zl, x, l):
    return r, zh, zl ^ 1, x, l ^ 1


def to_far_pair(r, zh, zl, x, l):
    return r, zh ^ 1, zl ^ 1, x, l


def to_row(r, zh, zl, x, l):
    return r ^ 1, zh, zl, x, l


def to_group(b1, b2):
    return lambda r, zh, zl, x, l: (r, zh ^ b1, zl, x ^ b2, l)


def to_group_by_core(b1, b2):
    return lambda r, zh, zl, x, l: (r ^ l, zh ^ b1, zl, x ^ b2, l)


def after(value, *others):
    return lax.optimization_barrier((value,) + others)[0]


def vmem():
    return pl.BlockSpec(memory_space=pltpu.VMEM)


def smem():
    return pl.BlockSpec(memory_space=pltpu.SMEM)


def shaped(*dims):
    return jax.ShapeDtypeStruct(dims, F32)


def lanes_low():
    return lax.broadcasted_iota(jnp.int32, (1, 128), 1) < 64


def swap_lanes(one, two):
    low = lanes_low()
    even = jnp.where(low, one, pltpu.roll(two, 64, one.ndim - 1))
    odd = jnp.where(low, pltpu.roll(one, 64, one.ndim - 1), two)
    return even, odd


def split(value):
    high = value.astype(BF16)
    return high, (value - high.astype(F32)).astype(BF16)


def dot3(left, right):
    lh, ll = left
    rh, rl = right
    whole = jnp.dot(lh, rl, preferred_element_type=F32)
    whole += jnp.dot(ll, rh, preferred_element_type=F32)
    return whole + jnp.dot(lh, rh, preferred_element_type=F32)


def flat(value):
    return jnp.concatenate([value[:64], value[64:]], axis=1)


def spot():
    row, col, core = (lax.axis_index(name) for name in AXES)
    return row, col // 4, (col // 2) % 2, col % 2, core


def call(name, kernel, outs, *operands, specs=None, scratch=()):
    specs = specs or [None] * len(operands)
    fixed = [
        pltpu.with_memory_space_constraint(o, pltpu.VMEM) if s is None else o
        for o, s in zip(operands, specs)
    ]
    return pl.pallas_call(
        kernel,
        out_shape=[pltpu.VMEM(dims, F32) for dims in outs],
        in_specs=[vmem() if s is None else s for s in specs],
        out_specs=[vmem() for _ in outs],
        scratch_shapes=list(scratch),
        compiler_params=pltpu.CompilerParams(vmem_limit_bytes=VMEM_OF_A_KERNEL),

        name=name,
    )(*fixed)


def cut_columns(source, held, base):
    r = spot()[0]
    for p in range(2):
        for z in range(2):
            start = pl.multiple_of((2 * r + z) * 128, 128)
            one = source[p, 0, :, pl.ds(start, 128)]
            two = source[p, 1, :, pl.ds(start, 128)]
            even, odd = swap_lanes(one, two)
            held[2 * z, base + p] = even
            held[2 * z + 1, base + p] = odd


def part_rows(source, keep, out):
    zl = spot()[2]
    for a in range(2):
        even, odd = swap_lanes(source[a, :, :128], source[a, :, 128:])
        keep[a] = jnp.where(zl == 0, even, odd)
        out[a] = jnp.where(zl == 0, odd, even)


def begin_kernel(tiles, *refs):
    sources, outs, places = refs[:6], refs[6:15], refs[15:21]
    cuts, sems = refs[21:]
    copies = [
        pltpu.make_async_copy(source, place, sems.at[k])
        for k, (source, place) in enumerate(zip(sources, places))
    ]
    for copy in copies:
        copy.start()
    leaf_inv, blocks, leaf_rhs, root_rhs, root_inv, lower = places
    away, first, rest, masked_out, lower_out = outs[:5]
    core = spot()[4]

    def mask(m, dest, base):
        for t in range(2):
            lanes = slice(t * 128, t * 128 + 128)
            weight = tiles[0, t, 0, m].astype(F32)
            for a in range(2):
                dest[base + t, a] = blocks[0, m, a, :, lanes] * weight

    copies[0].wait()
    part_rows(leaf_inv.at[0, 0], first.at[0], away.at[0])
    copies[1].wait()
    mask(0, first, 1)
    copies[2].wait()
    cut_columns(leaf_rhs.at[0], cuts, 0)
    copies[3].wait()
    cut_columns(root_rhs, cuts, 2)
    _, zh, _, x, _ = spot()
    for b1 in range(2):
        for b2 in range(2):
            outs[5 + b1 * 2 + b2][...] = cuts[(zh ^ b1) * 2 + (x ^ b2)]
    part_rows(leaf_inv.at[0, 1], rest.at[0], away.at[1])
    copies[4].wait()
    part_rows(root_inv.at[core], rest.at[1], away.at[2])
    copies[5].wait()
    for a in range(2):
        start = pl.multiple_of(core * 128, 128)
        lower_out[0, a] = lower[a, :, pl.ds(start, 128)]
    for m in range(1, 5):
        mask(m, masked_out, 2 * (m - 1))


def begin(pattern, *arrays):
    tiles = pattern.transpose(0, 2, 3, 1)
    outs = [(3, 2, 32, 128), (3, 2, 32, 128), (2, 2, 32, 128)] + [(8, 2, 32, 128), (1, 2, 32, 128)] + [(4, 32, 128)] * 4
    return pl.pallas_call(
        begin_kernel,
        out_shape=[pltpu.VMEM(dims, F32) for dims in outs],
        in_specs=[smem()] + [pl.BlockSpec(memory_space=pltpu.HBM)] * 6,
        out_specs=[vmem() for _ in outs],
        scratch_shapes=[pltpu.VMEM(a.shape, F32) for a in arrays]
        + [pltpu.VMEM((4, 4, 32, 128), F32), pltpu.SemaphoreType.DMA((6,))],
        compiler_params=pltpu.CompilerParams(vmem_limit_bytes=VMEM_OF_A_KERNEL),

        name="begin",
    )(tiles, *(pltpu.with_memory_space_constraint(a, pltpu.HBM) for a in arrays))


def fetch(pick, dest, sems, swapped=None, from_core=0):
    r, zh, _, x, l = spot()
    copies = []
    for b3 in range(2):
        for b2 in range(2):
            for b1 in range(2):

                def copy_of(source, core):
                    rr = r ^ jnp.where(core == 0, b3, b2)
                    xx = x ^ jnp.where(core == 0, b2, b3)
                    return pltpu.make_async_copy(
                        source(b3, b2, b1),
                        dest(rr, zh ^ b1, xx),
                        sems.at[b3 * 4 + b2 * 2 + b1],
                    )

                copy = copy_of(pick, l)
                if swapped is None:
                    copy.start()
                else:
                    pl.when(l == from_core)(copy.start)
                    pl.when(l != from_core)(copy_of(swapped, 1 - l).start)
                copies.append(copy)
    return copies


def wait_all(copies):
    for copy in copies:
        copy.wait()


def solve(inverse, vector):
    left = split(flat(vector))
    parts = [dot3(left, split(inverse[a].reshape(512, 128))) for a in range(2)]
    return jnp.concatenate(parts, axis=0)


def update(held, terms, waits):
    sums = [None, None]
    for t, vector in enumerate(terms):
        waits[t]()
        left = split(flat(vector))
        for a in range(2):
            right = jnp.concatenate(
                [held[t, a, 0].reshape(256, 128), held[t, a, 1].reshape(256, 128)], axis=1
            )
            part = dot3(left, split(right))
            sums[a] = part if sums[a] is None else sums[a] + part
    return jnp.concatenate(sums, axis=0)


def sum_four(refs):
    return (refs[0][...] + refs[2][...]) + (refs[1][...] + refs[3][...])


def first_chunk_unit(four, third):
    return lambda unit: lambda b3, b2, b1: (four, third)[b3].at[b2 * 2 + b1, unit]


def chunk_unit(near, far, start, far_start):
    def of(unit):
        def pick(b3, b2, b1):
            return (near, far)[b1][b3].at[b2, (start, far_start)[b1] + unit]

        return pick

    return of


def root_unit(ref):
    return lambda unit: lambda b3, b2, b1: ref.at[b1 * 4 + b3 * 2 + b2, unit]


def fetch_inverse(unit, inverse, sems, swapped=None, from_core=0):
    copies = []
    for half in range(2):
        copies += fetch(
            unit(half),
            lambda r, zh, x, half=half: inverse.at[r, :, zh, half, x],
            sems.at[half],
            swapped and swapped(half),
            from_core,
        )
    return copies


def fetch_block(unit, held, t, sems):
    copies = []
    for half in range(2):
        copies += fetch(
            unit(half), lambda r, zh, x, half=half: held.at[t, r, half, :, zh, x], sems.at[half]
        )
    return copies


def fetch_halves(root, swapped, held, t, sems):
    copies = []
    for half in range(2):
        copies += fetch(
            root(2),
            lambda r, zh, x, half=half: held.at[t, r, half, :, zh, x],
            sems.at[half],
            swapped(2),
            half,
        )
    return copies


def shifted(unit, by):
    return lambda half: unit(half + by)


def link_0_kernel(b_ref, four, third, part_ref, y_ref, inverse, held, sems):
    unit = first_chunk_unit(four, third)
    first = fetch_inverse(unit, inverse, sems.at[0])
    second = fetch_block(shifted(unit, 2), held, 0, sems.at[1])
    wait_all(first)
    solved = solve(inverse, b_ref[...])
    y_ref[...] = solved
    part_ref[...] = update(held, [solved], [functools.partial(wait_all, second)])


def link_1_kernel(b_ref, own, got, y0_ref, n0, n1, f0, f1, part_ref, y_ref, inverse, held, sems):
    unit = chunk_unit((n0, n1), (f0, f1), 0, 0)
    first = fetch_inverse(unit, inverse, sems.at[0])
    copies = [fetch_block(shifted(unit, 2 * t + 2), held, t, sems.at[t + 1]) for t in range(2)]
    wait_all(first)
    solved = solve(inverse, b_ref[...] - (own[...] + got[...]))
    y_ref[...] = solved
    waits = [functools.partial(wait_all, c) for c in copies]
    part_ref[...] = update(held, [y0_ref[...], solved], waits)


def link_2_kernel(b_ref, s0, s1, s2, s3, y0_ref, y1_ref, n0, n1, f0, f1, root, swapped, *refs):
    part_ref, y_ref, inverse, held, sems = refs
    unit = chunk_unit((n0, n1), (f0, f1), 9, 0)
    root, swapped = root_unit(root), root_unit(swapped)
    first = fetch_inverse(root, inverse, sems.at[0], swapped, 0)
    copies = [fetch_block(shifted(unit, 2 * t), held, t, sems.at[t + 1]) for t in range(2)]
    copies.append(fetch_halves(root, swapped, held, 2, sems.at[3]))
    wait_all(first)
    solved = solve(inverse, b_ref[...] - sum_four((s0, s1, s2, s3)))
    y_ref[...] = solved
    waits = [functools.partial(wait_all, c) for c in copies]
    last = jnp.where(spot()[4] == 0, solved, 0.0)
    part_ref[...] = update(held, [y0_ref[...], y1_ref[...], last], waits)


def link_3_kernel(b_ref, s0, s1, s2, s3, y0_ref, y1_ref, y2_ref, root, swapped, *refs):
    outs, (pieces, inverse, sems) = refs[:4], refs[4:]
    first = fetch_inverse(root_unit(root), inverse, sems.at[0], root_unit(swapped), 1)
    vector = b_ref[...] - sum_four((s0, s1, s2, s3))
    lay_values((y0_ref, y1_ref, y2_ref), pieces)
    wait_all(first)
    pieces[:, 3] = solve(inverse, vector).T.reshape(4, 32, 128)
    _, zh, _, x, _ = spot()
    for b1 in range(2):
        for b2 in range(2):
            outs[b1 * 2 + b2][...] = pieces[(zh ^ b1) * 2 + (x ^ b2)]


def link_scratch(nblocks, nsems):
    blocks = [pltpu.VMEM((nblocks, 2, 2, 2, 2, 2, 32, 128), F32)] if nblocks else []
    return (
        [pltpu.VMEM((2, 2, 2, 2, 2, 32, 128), F32)] + blocks + [pltpu.SemaphoreType.DMA((nsems, 2, 8))]
    )


def lay_values(refs, held):
    for p, ref in enumerate(refs):
        held[:, p] = ref[...].T.reshape(4, 32, 128)


def stand_kernel(near_ref, other_ref, *refs):
    outs, held = refs[:4], refs[4]
    _, zh, zl, x, _ = spot()
    for b1 in range(2):
        for b2 in range(2):
            for b, source in enumerate((near_ref, other_ref)):
                held[((zh ^ b1) * 2 + (zl ^ b)) * 2 + (x ^ b2)] = source[b1 * 2 + b2]
    for p, out in enumerate(outs):
        out[...] = held[:, p].reshape(256, 128).T


def join_kernel(near_ref, other_ref, out_ref, held):
    r, zh, _, x, core = spot()
    near = r ^ core
    for b1 in range(2):
        for b2 in range(2):
            place = (zh ^ b1) * 2 + (x ^ b2)
            held[near * 4 + place] = near_ref[b1 * 2 + b2]
            held[(near ^ 1) * 4 + place] = other_ref[b1 * 2 + b2]
    for p in range(2):
        for u in range(4):
            lanes = slice(u * 128, u * 128 + 128)
            out_ref[p, 0, :, lanes], out_ref[p, 1, :, lanes] = swap_lanes(
                held[2 * u, p], held[2 * u + 1, p]
            )


def join(name, near, other):
    return pl.pallas_call(
        join_kernel,
        out_shape=shaped(2, 2, 32, 512),
        in_specs=[vmem()] * 2,
        out_specs=vmem(),
        scratch_shapes=[pltpu.VMEM((8, 2, 32, 128), F32)],
        compiler_params=pltpu.CompilerParams(vmem_limit_bytes=VMEM_OF_A_KERNEL),

        name=name,
    )(*(pltpu.with_memory_space_constraint(v, pltpu.VMEM) for v in (near, other)))


def to_groups(parts):
    return [parts[0]] + [send(parts[k], to_group(k // 2, k % 2)) for k in (1, 2, 3)]


VECTOR = [(128, 256), (128, 128)]


def grouped(leaf_rhs, root_rhs, leaf_inverses, root_inverses, leaf_blocks, root_block, pattern):
    zl = (lax.axis_index("col") // 2) % 2

    def whole(keep, got):
        return jnp.stack([jnp.where(zl == 0, keep, got), jnp.where(zl == 0, got, keep)])

    away, first, rest, blocks, lower, *cuts = begin(
        pattern, leaf_inverses, leaf_blocks, leaf_rhs, root_rhs, root_inverses, root_block
    )
    pair = send(away, to_pair)
    first_far = send(first, to_far)
    first_far_pair = send(away[0], to_far_pair)

    def first_chunk(values, got):
        return jnp.concatenate([whole(values[0], got), values[1:]])

    moved = to_groups(cuts)
    two_a = jnp.stack([first_chunk(first, pair[0]), first_chunk(first_far, first_far_pair)])
    second_a = send(two_a, to_second)
    rhs_in = jnp.stack(after(moved, two_a))
    rhs_pair = send(rhs_in, to_pair)

    late = after(pair, rhs_in)
    own_units = jnp.concatenate(
        [whole(rest[0], late[1]), blocks[:4], whole(rest[1], late[2]), lower, blocks[4:]]
    )
    far_b = send(own_units[:9], to_far)
    second_own = send(own_units, to_second)
    four_a = jnp.concatenate([two_a, after(second_a, own_units)])
    third_a = send(four_a, to_third)
    near_0 = jnp.stack([own_units, after(second_own, third_a)])
    near_1 = send(near_0, to_third)
    far_b = after(far_b, third_a)
    second_b = send(far_b, to_second)
    far_c = send(after(own_units[9:], far_b), to_far)
    b0, b1, r2, r3 = call(
        "stand",
        stand_kernel,
        [(128, 256)] * 4,
        after(rhs_in, third_a),
        rhs_pair,
        scratch=[pltpu.VMEM((8, 4, 32, 128), F32)],
    )

    own, y0 = call(
        "link_0",
        link_0_kernel,
        VECTOR,
        after(b0, near_0, far_b),
        four_a,
        third_a,
        scratch=link_scratch(1, 2),
    )
    got = send(own, to_pair)
    far_b_0 = jnp.stack([far_b, after(second_b, got)])
    far_b_1 = send(far_b_0, to_third)
    far_c = after(far_c, far_b_0)
    second_c = send(far_c, to_second)
    far_c_0 = jnp.stack([far_c, second_c])
    far_c_1 = send(far_c_0, to_third)

    own, y1 = call(
        "link_1",
        link_1_kernel,
        VECTOR,
        after(b1, far_c_0),
        own,
        got,
        y0,
        near_0,
        near_1,
        far_b_0,
        far_b_1,
        scratch=link_scratch(2, 3),
    )
    sums = [own, send(own, to_core), send(own, to_pair), send(own, to_pair_core)]
    root_own = jnp.concatenate(
        [after(near_0[:, 6:9], own), near_1[:, 6:9], far_b_0[:, 6:9], far_b_1[:, 6:9]]
    )
    root_swapped = send(root_own, to_core)

    own, y2 = call(
        "link_2",
        link_2_kernel,
        VECTOR,
        r2,
        *sums,
        y0,
        y1,
        near_0,
        near_1,
        far_c_0,
        far_c_1,
        root_own,
        root_swapped,
        scratch=link_scratch(3, 4),
    )
    sums = [own, send(own, to_core), send(own, to_pair), send(own, to_pair_core)]
    parts = call(
        "link_3",
        link_3_kernel,
        [(4, 32, 128)] * 4,
        r3,
        *sums,
        y0,
        y1,
        y2,
        root_own,
        root_swapped,
        scratch=[pltpu.VMEM((4, 4, 32, 128), F32)] + link_scratch(0, 1),
    )
    moved = jnp.stack([send(parts[k], to_group_by_core(k // 2, k % 2)) for k in range(4)])
    leaf_near, root_near = moved[:, :2], moved[:, 2:]
    leaf_other = send(leaf_near, to_row)
    root_other = send(root_near, to_core)
    return (
        join("join_leaf", leaf_near, leaf_other)[None],
        join("join_root", root_near, root_other),
    )


def solution(mesh):
    placed = (
        P("leaf", None, None, "col", None),
        P(None, None, "col", None),
        P("leaf", None, None, "col", "row"),
        P(None, None, "col", "row"),
        P("leaf", None, None, "col", "row"),
        P(None, "col", "row"),
        P("leaf", None, "row", "col"),
    )
    small = (mesh.shape["row"], mesh.shape["col"], mesh.shape["leaf"]) == (2, 8, 2)
    return jax.shard_map(
        grouped if small else general,
        mesh=mesh,
        in_specs=placed,
        out_specs=(P("leaf", None, None, "col", None), P(None, None, "col", None)),
        check_vma=False,
    )
```

```python
import functools

import jax
import jax.numpy as jnp
from jax import lax
from jax.experimental import pallas as pl
from jax.experimental.pallas import tpu as pltpu
from jax.sharding import PartitionSpec as P

BLK = 128
AXES = ("row", "col", "leaf")
F32 = jnp.float32
BF16 = jnp.bfloat16
VMEM_OF_A_KERNEL = 16 * 2**20


def apply_rows(block, vector):
    block = block.reshape(-1, block.shape[-1])
    vector = vector.reshape(-1, vector.shape[-1])
    term = lax.dot_general(
        block,
        vector,
        (((0,), (0,)), ((), ())),
        precision=lax.Precision.HIGHEST,
        preferred_element_type=F32,
    )
    owned = lax.psum_scatter(term, "col", scatter_dimension=0, tiled=True)
    return lax.all_gather(owned[None], "row", axis=0, tiled=True)


def masked(leaf_blocks, pattern):
    local = leaf_blocks[0]
    shaped = local.reshape(local.shape[:3] + (local.shape[3] // BLK, BLK))
    weights = pattern[0].astype(F32).transpose(0, 2, 1)[:, None, :, :, None]
    return (shaped * weights).reshape(local.shape)


def general(leaf_rhs, root_rhs, leaf_inverses, root_inverses, leaf_blocks, root_block, pattern):
    blocks = masked(leaf_blocks, pattern)
    first = apply_rows(leaf_inverses[0, 0], leaf_rhs[0, 0])
    second = apply_rows(leaf_inverses[0, 1], leaf_rhs[0, 1] - apply_rows(blocks[0], first))
    upper_two = apply_rows(blocks[1], first) + apply_rows(blocks[2], second)
    upper_three = apply_rows(blocks[3], first) + apply_rows(blocks[4], second)
    upper_two, upper_three = lax.psum((upper_two, upper_three), "leaf")
    third = apply_rows(root_inverses[0], root_rhs[0] - upper_two)
    fourth = apply_rows(root_inverses[1], root_rhs[1] - upper_three - apply_rows(root_block, third))
    return (jnp.stack([first, second])[None], jnp.stack([third, fourth]))


def pairs(dest):
    def place(r, z, side, x, l):
        return (r * 8 + side * 4 + z * 2 + x) * 2 + l

    every = [
        (r, z, side, x, l)
        for r in range(2)
        for z in range(2)
        for side in range(2)
        for x in range(2)
        for l in range(2)
    ]
    return sorted((place(*d), place(*dest(*d))) for d in every)


def send(value, dest):
    return lax.ppermute(value, AXES, pairs(dest))


def to_far(r, z, side, x, l):
    return r, z ^ 1, side, x, l


def to_second(r, z, side, x, l):
    return (r, z, side, x ^ 1, l) if l == 0 else (r ^ 1, z, side, x, l)


def to_third(r, z, side, x, l):
    return (r ^ 1, z, side, x, l) if l == 0 else (r, z, side, x ^ 1, l)


def to_pair(r, z, side, x, l):
    return r, z, side ^ 1, x, l


def to_core(r, z, side, x, l):
    return r, z, side, x, l ^ 1


def to_pair_core(r, z, side, x, l):
    return r, z, side ^ 1, x, l ^ 1


def to_far_pair(r, z, side, x, l):
    return r, z ^ 1, side ^ 1, x, l


def to_row(r, z, side, x, l):
    return r ^ 1, z, side, x, l


def to_group(b1, b2):
    return lambda r, z, side, x, l: (r, z ^ b1, side, x ^ b2, l)


def to_group_by_core(b1, b2):
    return lambda r, z, side, x, l: (r ^ l, z ^ b1, side, x ^ b2, l)


def after(value, *others):
    return lax.optimization_barrier((value,) + others)[0]


def vmem():
    return pl.BlockSpec(memory_space=pltpu.VMEM)


def smem():
    return pl.BlockSpec(memory_space=pltpu.SMEM)


def shaped(*dims):
    return jax.ShapeDtypeStruct(dims, F32)


def lanes_low():
    return lax.broadcasted_iota(jnp.int32, (1, 128), 1) < 64


def swap_lanes(one, two):
    low = lanes_low()
    even = jnp.where(low, one, pltpu.roll(two, 64, one.ndim - 1))
    odd = jnp.where(low, pltpu.roll(one, 64, one.ndim - 1), two)
    return even, odd


def split(value):
    high = value.astype(BF16)
    return high, (value - high.astype(F32)).astype(BF16)


def dot3(left, right):
    lh, ll = left
    rh, rl = right
    whole = jnp.dot(lh, rl, preferred_element_type=F32)
    whole += jnp.dot(ll, rh, preferred_element_type=F32)
    return whole + jnp.dot(lh, rh, preferred_element_type=F32)


def flat(value):
    return jnp.concatenate([value[:64], value[64:]], axis=1)


def spot():
    row, col, core = (lax.axis_index(name) for name in AXES)
    return row, (col // 2) % 2, col // 4, col % 2, core


def call(name, kernel, outs, *operands, specs=None, scratch=()):
    specs = specs or [None] * len(operands)
    fixed = [
        pltpu.with_memory_space_constraint(o, pltpu.VMEM) if s is None else o
        for o, s in zip(operands, specs)
    ]
    return pl.pallas_call(
        kernel,
        out_shape=[pltpu.VMEM(dims, F32) for dims in outs],
        in_specs=[vmem() if s is None else s for s in specs],
        out_specs=[vmem() for _ in outs],
        scratch_shapes=list(scratch),
        compiler_params=pltpu.CompilerParams(vmem_limit_bytes=VMEM_OF_A_KERNEL),
        name=name,
    )(*fixed)


def cut_columns(source, held, base):
    r = spot()[0]
    for p in range(2):
        for z in range(2):
            start = pl.multiple_of((2 * r + z) * 128, 128)
            one = source[p, 0, :, pl.ds(start, 128)]
            two = source[p, 1, :, pl.ds(start, 128)]
            even, odd = swap_lanes(one, two)
            held[2 * z, base + p] = even
            held[2 * z + 1, base + p] = odd


def part_rows(source, keep, out):
    side = spot()[2]
    mine = pl.multiple_of(side * 128, 128)
    theirs = pl.multiple_of((1 - side) * 128, 128)
    for a in range(2):
        keep[a] = source[a, :, pl.ds(mine, 128)]
        out[a] = source[a, :, pl.ds(theirs, 128)]


def begin_kernel(tiles, *refs):
    sources, outs, places = refs[:6], refs[6:16], refs[16:22]
    cuts, sems = refs[22:]
    copies = [
        pltpu.make_async_copy(source, place, sems.at[k])
        for k, (source, place) in enumerate(zip(sources, places))
    ]
    for copy in copies:
        copy.start()
    leaf_inv, blocks, leaf_rhs, root_rhs, root_inv, lower = places
    away, first, rest_away, rest, masked_out, lower_out = outs[:6]
    core = spot()[4]

    def mask(m, dest, base):
        for t in range(2):
            lanes = slice(t * 128, t * 128 + 128)
            weight = tiles[0, t, 0, m].astype(F32)
            for a in range(2):
                dest[base + t, a] = blocks[0, m, a, :, lanes] * weight

    copies[0].wait()
    part_rows(leaf_inv.at[0, 0], first.at[0], away)
    copies[1].wait()
    mask(0, first, 1)
    copies[2].wait()
    cut_columns(leaf_rhs.at[0], cuts, 0)
    copies[3].wait()
    cut_columns(root_rhs, cuts, 2)
    _, z, _, x, _ = spot()
    for b1 in range(2):
        for b2 in range(2):
            outs[6 + b1 * 2 + b2][...] = cuts[(z ^ b1) * 2 + (x ^ b2)]
    part_rows(leaf_inv.at[0, 1], rest.at[0], rest_away.at[0])
    copies[4].wait()
    part_rows(root_inv.at[core], rest.at[1], rest_away.at[1])
    copies[5].wait()
    for a in range(2):
        start = pl.multiple_of(core * 128, 128)
        lower_out[0, a] = lower[a, :, pl.ds(start, 128)]
    for m in range(1, 5):
        mask(m, masked_out, 2 * (m - 1))


def begin(pattern, *arrays):
    tiles = pattern.transpose(0, 2, 3, 1)
    outs = [(2, 32, 128), (3, 2, 32, 128), (2, 2, 32, 128), (2, 2, 32, 128)] + [(8, 2, 32, 128), (1, 2, 32, 128)] + [(4, 32, 128)] * 4
    return pl.pallas_call(
        begin_kernel,
        out_shape=[pltpu.VMEM(dims, F32) for dims in outs],
        in_specs=[smem()] + [pl.BlockSpec(memory_space=pltpu.HBM)] * 6,
        out_specs=[vmem() for _ in outs],
        scratch_shapes=[pltpu.VMEM(a.shape, F32) for a in arrays]
        + [pltpu.VMEM((4, 4, 32, 128), F32), pltpu.SemaphoreType.DMA((6,))],
        compiler_params=pltpu.CompilerParams(vmem_limit_bytes=VMEM_OF_A_KERNEL),
        name="begin",
    )(tiles, *(pltpu.with_memory_space_constraint(a, pltpu.HBM) for a in arrays))


def fetch(pick, dest, sems, swapped=None, from_core=0):
    r, z, _, x, l = spot()
    copies = []
    for b3 in range(2):
        for b2 in range(2):
            for b1 in range(2):

                def copy_of(source, core):
                    rr = r ^ jnp.where(core == 0, b3, b2)
                    xx = x ^ jnp.where(core == 0, b2, b3)
                    return pltpu.make_async_copy(
                        source(b3, b2, b1),
                        dest(rr, z ^ b1, xx),
                        sems.at[b3 * 4 + b2 * 2 + b1],
                    )

                copy = copy_of(pick, l)
                if swapped is None:
                    copy.start()
                else:
                    pl.when(l == from_core)(copy.start)
                    pl.when(l != from_core)(copy_of(swapped, 1 - l).start)
                copies.append(copy)
    return copies


def wait_all(copies):
    for copy in copies:
        copy.wait()


def solve(inverse, vector):
    left = split(flat(vector))
    parts = [dot3(left, split(inverse[a].reshape(512, 128))) for a in range(2)]
    return jnp.concatenate(parts, axis=0)


def update(held, terms, waits):
    sums = [None, None]
    for t, vector in enumerate(terms):
        waits[t]()
        left = split(flat(vector))
        for a in range(2):
            right = jnp.concatenate(
                [held[t, a, 0].reshape(256, 128), held[t, a, 1].reshape(256, 128)], axis=1
            )
            part = dot3(left, split(right))
            sums[a] = part if sums[a] is None else sums[a] + part
    return jnp.concatenate(sums, axis=0)


def first_chunk_unit(four, third):
    return lambda unit: lambda b3, b2, b1: (four, third)[b3].at[b2 * 2 + b1, unit]


def chunk_unit(near, far, start, far_start):
    def of(unit):
        def pick(b3, b2, b1):
            return (near, far)[b1][b3].at[b2, (start, far_start)[b1] + unit]

        return pick

    return of


def root_unit(ref):
    return lambda unit: lambda b3, b2, b1: ref.at[b1 * 4 + b3 * 2 + b2, unit]


def fetch_inverse(unit, inverse, sems, swapped=None, from_core=0):
    copies = []
    for half in range(2):
        copies += fetch(
            unit(half),
            lambda r, z, x, half=half: inverse.at[r, :, half, z, x],
            sems.at[half],
            swapped and swapped(half),
            from_core,
        )
    return copies


def fetch_block(unit, held, t, sems):
    copies = []
    for half in range(2):
        copies += fetch(
            unit(half), lambda r, z, x, half=half: held.at[t, r, half, :, z, x], sems.at[half]
        )
    return copies


def fetch_halves(root, swapped, held, t, sems):
    copies = []
    for half in range(2):
        copies += fetch(
            root(2),
            lambda r, z, x, half=half: held.at[t, r, half, :, z, x],
            sems.at[half],
            swapped(2),
            half,
        )
    return copies


def shifted(unit, by):
    return lambda half: unit(half + by)


def link_0_kernel(b_ref, four, third, part_ref, y_ref, inverse, held, sems):
    unit = first_chunk_unit(four, third)
    first = fetch_inverse(unit, inverse, sems.at[0])
    second = fetch_block(shifted(unit, 2), held, 0, sems.at[1])
    wait_all(first)
    solved = solve(inverse, b_ref[...])
    y_ref[...] = solved
    part_ref[...] = update(held, [solved], [functools.partial(wait_all, second)])


def link_1_kernel(b_ref, own, got, y0_ref, n0, n1, f0, f1, part_ref, y_ref, inverse, held, sems):
    unit = chunk_unit((n0, n1), (f0, f1), 0, 0)
    first = fetch_inverse(unit, inverse, sems.at[0])
    copies = [fetch_block(shifted(unit, 2 * t + 2), held, t, sems.at[t + 1]) for t in range(2)]
    wait_all(first)
    solved = solve(inverse, b_ref[...] - (own[...] + got[...]))
    y_ref[...] = solved
    waits = [functools.partial(wait_all, c) for c in copies]
    part_ref[...] = update(held, [y0_ref[...], solved], waits)


def link_2_kernel(b_ref, s0, s1, y0_ref, y1_ref, n0, n1, f0, f1, root, swapped, *refs):
    part_ref, y_ref, inverse, held, sems = refs
    unit = chunk_unit((n0, n1), (f0, f1), 9, 0)
    root, swapped = root_unit(root), root_unit(swapped)
    first = fetch_inverse(root, inverse, sems.at[0], swapped, 0)
    copies = [fetch_block(shifted(unit, 2 * t), held, t, sems.at[t + 1]) for t in range(2)]
    copies.append(fetch_halves(root, swapped, held, 2, sems.at[3]))
    wait_all(first)
    solved = solve(inverse, b_ref[...] - (s0[...] + s1[...]))
    y_ref[...] = solved
    waits = [functools.partial(wait_all, c) for c in copies]
    last = jnp.where(spot()[4] == 0, solved, 0.0)
    part_ref[...] = update(held, [y0_ref[...], y1_ref[...], last], waits)


def link_3_kernel(b_ref, s0, s1, y0_ref, y1_ref, y2_ref, root, swapped, *refs):
    outs, (pieces, inverse, sems) = refs[:4], refs[4:]
    first = fetch_inverse(root_unit(root), inverse, sems.at[0], root_unit(swapped), 1)
    vector = b_ref[...] - (s0[...] + s1[...])
    lay_values((y0_ref, y1_ref, y2_ref), pieces)
    wait_all(first)
    pieces[:, 3] = solve(inverse, vector).T.reshape(4, 32, 128)
    _, z, _, x, _ = spot()
    for b1 in range(2):
        for b2 in range(2):
            outs[b1 * 2 + b2][...] = pieces[(z ^ b1) * 2 + (x ^ b2)]


def link_scratch(nblocks, nsems):
    blocks = [pltpu.VMEM((nblocks, 2, 2, 2, 2, 2, 32, 128), F32)] if nblocks else []
    return (
        [pltpu.VMEM((2, 2, 2, 2, 2, 32, 128), F32)] + blocks + [pltpu.SemaphoreType.DMA((nsems, 2, 8))]
    )


def root_kernel(n0, n1, f0, f1, _, out):
    for k, ref in enumerate((n0, n1, f0, f1)):
        for b2 in range(2):
            for unit in range(3):
                out[2 * k + b2, unit] = ref[b2, 6 + unit]


def lay_values(refs, held):
    for p, ref in enumerate(refs):
        held[:, p] = ref[...].T.reshape(4, 32, 128)


def stand_kernel(near_ref, other_ref, *refs):
    outs, held = refs[:2], refs[2]
    _, z, side, x, _ = spot()
    for b1 in range(2):
        for b2 in range(2):
            for b, source in enumerate((near_ref, other_ref)):
                held[((side ^ b) * 2 + (z ^ b1)) * 2 + (x ^ b2)] = source[b1 * 2 + b2]
    for p, out in enumerate(outs):
        out[...] = held[:, p].reshape(256, 128).T


def join_kernel(near_ref, other_ref, out_ref, held):
    r, z, _, x, core = spot()
    near = r ^ core
    for b1 in range(2):
        for b2 in range(2):
            place = (z ^ b1) * 2 + (x ^ b2)
            held[near * 4 + place] = near_ref[b1 * 2 + b2]
            held[(near ^ 1) * 4 + place] = other_ref[b1 * 2 + b2]
    for p in range(2):
        for u in range(4):
            lanes = slice(u * 128, u * 128 + 128)
            out_ref[p, 0, :, lanes], out_ref[p, 1, :, lanes] = swap_lanes(
                held[2 * u, p], held[2 * u + 1, p]
            )


def join(name, near, other):
    return pl.pallas_call(
        join_kernel,
        out_shape=shaped(2, 2, 32, 512),
        in_specs=[vmem()] * 2,
        out_specs=vmem(),
        scratch_shapes=[pltpu.VMEM((8, 2, 32, 128), F32)],
        compiler_params=pltpu.CompilerParams(vmem_limit_bytes=VMEM_OF_A_KERNEL),
        name=name,
    )(*(pltpu.with_memory_space_constraint(v, pltpu.VMEM) for v in (near, other)))


def to_groups(parts):
    return [parts[0]] + [send(parts[k], to_group(k // 2, k % 2)) for k in (1, 2, 3)]


VECTOR = [(128, 256), (128, 128)]


def grouped(leaf_rhs, root_rhs, leaf_inverses, root_inverses, leaf_blocks, root_block, pattern):
    side = lax.axis_index("col") // 4
    standing = [pltpu.VMEM((8, 2, 32, 128), F32)]

    def whole(keep, got):
        return jnp.stack([jnp.where(side == 0, keep, got), jnp.where(side == 0, got, keep)])

    def first_chunk(values, got):
        return jnp.concatenate([whole(values[0], got), values[1:]])

    away, first, rest_away, rest, blocks, lower, *cuts = begin(
        pattern, leaf_inverses, leaf_blocks, leaf_rhs, root_rhs, root_inverses, root_block
    )
    first_pair = send(away, to_pair)
    first_far = send(first, to_far)
    first_far_pair = send(away, to_far_pair)
    rest_pair = send(rest_away, to_pair)
    moved = to_groups(cuts)

    two_a = jnp.stack([first_chunk(first, first_pair), first_chunk(first_far, first_far_pair)])
    second_a = send(two_a, to_second)
    rhs_in = jnp.stack(after(moved, two_a))
    leaf_pair = send(rhs_in[:, :2], to_pair)

    late = after(rest_pair, rhs_in)
    own_units = jnp.concatenate(
        [whole(rest[0], late[0]), blocks[:4], whole(rest[1], late[1]), lower, blocks[4:]]
    )
    far_b = send(own_units[:9], to_far)
    second_own = send(own_units, to_second)
    four_a = jnp.concatenate([two_a, after(second_a, own_units)])
    third_a = send(four_a, to_third)
    near_0 = jnp.stack([own_units, after(second_own, third_a)])
    near_1 = send(near_0, to_third)
    far_b = after(far_b, third_a)
    second_b = send(far_b, to_second)
    far_c = send(after(own_units[9:], far_b), to_far)
    b0, b1 = call(
        "stand_leaf",
        stand_kernel,
        [(128, 256)] * 2,
        after(rhs_in[:, :2], third_a),
        leaf_pair,
        scratch=standing,
    )

    own, y0 = call(
        "link_0",
        link_0_kernel,
        VECTOR,
        after(b0, near_0, far_b),
        four_a,
        third_a,
        scratch=link_scratch(1, 2),
    )
    got = send(own, to_pair)
    far_b_0 = jnp.stack([far_b, after(second_b, got)])
    far_b_1 = send(far_b_0, to_third)
    far_c = after(far_c, far_b_0)
    second_c = send(far_c, to_second)
    root_in = after(rhs_in[:, 2:], far_b_0)
    root_pair = send(root_in, to_pair)
    far_c_0 = jnp.stack([far_c, second_c])
    far_c_1 = send(far_c_0, to_third)

    own, y1 = call(
        "link_1",
        link_1_kernel,
        VECTOR,
        after(b1, far_c_0),
        own,
        got,
        y0,
        near_0,
        near_1,
        far_b_0,
        far_b_1,
        scratch=link_scratch(2, 3),
    )
    both = own + send(own, to_core)
    got = send(both, to_pair)
    (root_own,) = call(
        "root_shards", root_kernel, [(8, 3, 2, 32, 128)], near_0, near_1, far_b_0, far_b_1, both
    )
    root_swapped = send(root_own, to_core)
    r2, r3 = call(
        "stand_root",
        stand_kernel,
        [(128, 256)] * 2,
        after(root_in, both),
        root_pair,
        scratch=standing,
    )

    own, y2 = call(
        "link_2",
        link_2_kernel,
        VECTOR,
        r2,
        both,
        got,
        y0,
        y1,
        near_0,
        near_1,
        far_c_0,
        far_c_1,
        root_own,
        root_swapped,
        scratch=link_scratch(3, 4),
    )
    both = own + send(own, to_core)
    got = send(both, to_pair)

    parts = call(
        "link_3",
        link_3_kernel,
        [(4, 32, 128)] * 4,
        r3,
        both,
        got,
        y0,
        y1,
        y2,
        root_own,
        root_swapped,
        scratch=[pltpu.VMEM((4, 4, 32, 128), F32)] + link_scratch(0, 1),
    )
    moved = jnp.stack([send(parts[k], to_group_by_core(k // 2, k % 2)) for k in range(4)])
    leaf_near, root_near = moved[:, :2], moved[:, 2:]
    leaf_other = send(leaf_near, to_row)
    root_other = send(root_near, to_core)
    return (
        join("join_leaf", leaf_near, leaf_other)[None],
        join("join_root", root_near, root_other),
    )


def solution(mesh):
    placed = (
        P("leaf", None, None, "col", None),
        P(None, None, "col", None),
        P("leaf", None, None, "col", "row"),
        P(None, None, "col", "row"),
        P("leaf", None, None, "col", "row"),
        P(None, "col", "row"),
        P("leaf", None, "row", "col"),
    )
    small = (mesh.shape["row"], mesh.shape["col"], mesh.shape["leaf"]) == (2, 8, 2)
    return jax.shard_map(
        grouped if small else general,
        mesh=mesh,
        in_specs=placed,
        out_specs=(P("leaf", None, None, "col", None), P(None, None, "col", None)),
        check_vma=False,
    )
```

```python
import functools

import jax
import jax.numpy as jnp
from jax import lax
from jax.experimental import pallas as pl
from jax.experimental.pallas import tpu as pltpu
from jax.sharding import PartitionSpec as P

BLK = 128
AXES = ("row", "col", "leaf")
F32 = jnp.float32
BF16 = jnp.bfloat16
VMEM_OF_A_KERNEL = 16 * 2**20


def apply_rows(block, vector):
    block = block.reshape(-1, block.shape[-1])
    vector = vector.reshape(-1, vector.shape[-1])
    term = lax.dot_general(
        block,
        vector,
        (((0,), (0,)), ((), ())),
        precision=lax.Precision.HIGHEST,
        preferred_element_type=F32,
    )
    owned = lax.psum_scatter(term, "col", scatter_dimension=0, tiled=True)
    return lax.all_gather(owned[None], "row", axis=0, tiled=True)


def masked(leaf_blocks, pattern):
    local = leaf_blocks[0]
    shaped = local.reshape(local.shape[:3] + (local.shape[3] // BLK, BLK))
    weights = pattern[0].astype(F32).transpose(0, 2, 1)[:, None, :, :, None]
    return (shaped * weights).reshape(local.shape)


def general(leaf_rhs, root_rhs, leaf_inverses, root_inverses, leaf_blocks, root_block, pattern):
    blocks = masked(leaf_blocks, pattern)
    first = apply_rows(leaf_inverses[0, 0], leaf_rhs[0, 0])
    second = apply_rows(leaf_inverses[0, 1], leaf_rhs[0, 1] - apply_rows(blocks[0], first))
    upper_two = apply_rows(blocks[1], first) + apply_rows(blocks[2], second)
    upper_three = apply_rows(blocks[3], first) + apply_rows(blocks[4], second)
    upper_two, upper_three = lax.psum((upper_two, upper_three), "leaf")
    third = apply_rows(root_inverses[0], root_rhs[0] - upper_two)
    fourth = apply_rows(root_inverses[1], root_rhs[1] - upper_three - apply_rows(root_block, third))
    return (jnp.stack([first, second])[None], jnp.stack([third, fourth]))


def pairs(dest):
    out = []
    for r in range(2):
        for zh in range(2):
            for zl in range(2):
                for x in range(2):
                    for l in range(2):
                        d = dest(r, zh, zl, x, l)
                        if d is None:
                            continue
                        s = (r * 8 + zh * 4 + zl * 2 + x) * 2 + l
                        e = (d[0] * 8 + d[1] * 4 + d[2] * 2 + d[3]) * 2 + d[4]
                        out.append((s, e))
    return out


def send(value, dest):
    return lax.ppermute(value, AXES, pairs(dest))


def to_far(r, zh, zl, x, l):
    return r, zh ^ 1, zl, x, l


def to_second(r, zh, zl, x, l):
    return (r, zh, zl, x ^ 1, l) if l == 0 else (r ^ 1, zh, zl, x, l)


def to_third(r, zh, zl, x, l):
    return (r ^ 1, zh, zl, x, l) if l == 0 else (r, zh, zl, x ^ 1, l)


def to_pair(r, zh, zl, x, l):
    return r, zh, zl ^ 1, x, l


def to_core(r, zh, zl, x, l):
    return r, zh, zl, x, l ^ 1


def to_pair_core(r, zh, zl, x, l):
    return r, zh, zl ^ 1, x, l ^ 1


def to_far_pair(r, zh, zl, x, l):
    return r, zh ^ 1, zl ^ 1, x, l


def to_row(r, zh, zl, x, l):
    return r ^ 1, zh, zl, x, l


def to_group(b1, b2):
    return lambda r, zh, zl, x, l: (r, zh ^ b1, zl, x ^ b2, l)


def to_group_by_core(b1, b2):
    return lambda r, zh, zl, x, l: (r ^ l, zh ^ b1, zl, x ^ b2, l)


def after(value, *others):
    return lax.optimization_barrier((value,) + others)[0]


def vmem():
    return pl.BlockSpec(memory_space=pltpu.VMEM)


def smem():
    return pl.BlockSpec(memory_space=pltpu.SMEM)


def shaped(*dims):
    return jax.ShapeDtypeStruct(dims, F32)


def lanes_low():
    return lax.broadcasted_iota(jnp.int32, (1, 128), 1) < 64


def swap_lanes(one, two):
    low = lanes_low()
    even = jnp.where(low, one, pltpu.roll(two, 64, one.ndim - 1))
    odd = jnp.where(low, pltpu.roll(one, 64, one.ndim - 1), two)
    return even, odd


def split(value):
    high = value.astype(BF16)
    return high, (value - high.astype(F32)).astype(BF16)


def dot3(left, right):
    lh, ll = left
    rh, rl = right
    whole = jnp.dot(lh, rl, preferred_element_type=F32)
    whole += jnp.dot(ll, rh, preferred_element_type=F32)
    return whole + jnp.dot(lh, rh, preferred_element_type=F32)


def flat(value):
    return jnp.concatenate([value[:64], value[64:]], axis=1)


def spot():
    row, col, core = (lax.axis_index(name) for name in AXES)
    return row, col // 4, (col // 2) % 2, col % 2, core


def call(name, kernel, outs, *operands, specs=None, scratch=()):
    specs = specs or [None] * len(operands)
    fixed = [
        pltpu.with_memory_space_constraint(o, pltpu.VMEM) if s is None else o
        for o, s in zip(operands, specs)
    ]
    return pl.pallas_call(
        kernel,
        out_shape=[pltpu.VMEM(dims, F32) for dims in outs],
        in_specs=[vmem() if s is None else s for s in specs],
        out_specs=[vmem() for _ in outs],
        scratch_shapes=list(scratch),
        compiler_params=pltpu.CompilerParams(vmem_limit_bytes=VMEM_OF_A_KERNEL),

        name=name,
    )(*fixed)


def cut_columns(source, held, base):
    r = spot()[0]
    for p in range(2):
        for z in range(2):
            start = pl.multiple_of((2 * r + z) * 128, 128)
            one = source[p, 0, :, pl.ds(start, 128)]
            two = source[p, 1, :, pl.ds(start, 128)]
            even, odd = swap_lanes(one, two)
            held[2 * z, base + p] = even
            held[2 * z + 1, base + p] = odd


def part_rows(source, keep, out):
    zl = spot()[2]
    for a in range(2):
        even, odd = swap_lanes(source[a, :, :128], source[a, :, 128:])
        keep[a] = jnp.where(zl == 0, even, odd)
        out[a] = jnp.where(zl == 0, odd, even)


def begin_kernel(tiles, *refs):
    sources, outs, places = refs[:6], refs[6:13], refs[13:19]
    cuts, sems = refs[19:]
    copies = [
        pltpu.make_async_copy(source, place, sems.at[k])
        for k, (source, place) in enumerate(zip(sources, places))
    ]
    for copy in copies:
        copy.start()
    leaf_inv, blocks, leaf_rhs, root_rhs, root_inv, lower = places
    away, first, masked_out = outs[:3]
    core = spot()[4]

    def mask(m, dest, base):
        for t in range(2):
            lanes = slice(t * 128, t * 128 + 128)
            weight = tiles[0, t, 0, m].astype(F32)
            for a in range(2):
                dest[base + t, a] = blocks[0, m, a, :, lanes] * weight

    copies[0].wait()
    part_rows(leaf_inv.at[0, 0], first.at[0], away.at[0])
    copies[1].wait()
    mask(0, first, 1)
    copies[2].wait()
    cut_columns(leaf_rhs.at[0], cuts, 0)
    copies[3].wait()
    cut_columns(root_rhs, cuts, 2)
    _, zh, _, x, _ = spot()
    for b1 in range(2):
        for b2 in range(2):
            outs[3 + b1 * 2 + b2][...] = cuts[(zh ^ b1) * 2 + (x ^ b2)]
    part_rows(leaf_inv.at[0, 1], first.at[3], away.at[1])
    copies[4].wait()
    part_rows(root_inv.at[core], first.at[4], away.at[2])
    copies[5].wait()
    for a in range(2):
        start = pl.multiple_of(core * 128, 128)
        masked_out[8, a] = lower[a, :, pl.ds(start, 128)]
    for m in range(1, 5):
        mask(m, masked_out, 2 * (m - 1))


def begin(pattern, *arrays):
    tiles = pattern.transpose(0, 2, 3, 1)
    outs = [(3, 2, 32, 128), (5, 2, 32, 128), (9, 2, 32, 128)] + [(4, 32, 128)] * 4
    return pl.pallas_call(
        begin_kernel,
        out_shape=[pltpu.VMEM(dims, F32) for dims in outs],
        in_specs=[smem()] + [pl.BlockSpec(memory_space=pltpu.HBM)] * 6,
        out_specs=[vmem() for _ in outs],
        scratch_shapes=[pltpu.VMEM(a.shape, F32) for a in arrays]
        + [pltpu.VMEM((4, 4, 32, 128), F32), pltpu.SemaphoreType.DMA((6,))],
        compiler_params=pltpu.CompilerParams(vmem_limit_bytes=VMEM_OF_A_KERNEL),

        name="begin",
    )(tiles, *(pltpu.with_memory_space_constraint(a, pltpu.HBM) for a in arrays))


def fetch(pick, dest, sems, swapped=None, from_core=0):
    r, zh, _, x, l = spot()
    copies = []
    for b3 in range(2):
        for b2 in range(2):
            for b1 in range(2):

                def copy_of(source, core):
                    rr = r ^ jnp.where(core == 0, b3, b2)
                    xx = x ^ jnp.where(core == 0, b2, b3)
                    return pltpu.make_async_copy(
                        source(b3, b2, b1),
                        dest(rr, zh ^ b1, xx),
                        sems.at[b3 * 4 + b2 * 2 + b1],
                    )

                copy = copy_of(pick, l)
                if swapped is None:
                    copy.start()
                else:
                    pl.when(l == from_core)(copy.start)
                    pl.when(l != from_core)(copy_of(swapped, 1 - l).start)
                copies.append(copy)
    return copies


def wait_all(copies):
    for copy in copies:
        copy.wait()


def solve(inverse, vector):
    left = split(flat(vector))
    parts = [dot3(left, split(inverse[a].reshape(512, 128))) for a in range(2)]
    return jnp.concatenate(parts, axis=0)


def update(held, terms, waits):
    sums = [None, None]
    for t, vector in enumerate(terms):
        waits[t]()
        left = split(flat(vector))
        for a in range(2):
            right = jnp.concatenate(
                [held[t, a, 0].reshape(256, 128), held[t, a, 1].reshape(256, 128)], axis=1
            )
            part = dot3(left, split(right))
            sums[a] = part if sums[a] is None else sums[a] + part
    return jnp.concatenate(sums, axis=0)


def sum_four(refs):
    return (refs[0][...] + refs[2][...]) + (refs[1][...] + refs[3][...])


def first_chunk_unit(four, third):
    return lambda unit: lambda b3, b2, b1: (four, third)[b3].at[b2 * 2 + b1, unit]


def block_unit(near, far):
    return lambda unit: lambda b3, b2, b1: (near, far)[b1][b3].at[b2, unit]


def root_unit(ref):
    return lambda unit: lambda b3, b2, b1: ref.at[b1 * 4 + b3 * 2 + b2, unit]


def fetch_inverse(unit, inverse, sems, swapped=None, from_core=0):
    copies = []
    for half in range(2):
        copies += fetch(
            unit(half),
            lambda r, zh, x, half=half: inverse.at[r, :, zh, half, x],
            sems.at[half],
            swapped and swapped(half),
            from_core,
        )
    return copies


def fetch_block(unit, held, t, sems):
    copies = []
    for half in range(2):
        copies += fetch(
            unit(half), lambda r, zh, x, half=half: held.at[t, r, half, :, zh, x], sems.at[half]
        )
    return copies


def fetch_halves(root, swapped, held, t, sems):
    copies = []
    for half in range(2):
        copies += fetch(
            root(2),
            lambda r, zh, x, half=half: held.at[t, r, half, :, zh, x],
            sems.at[half],
            swapped(2),
            half,
        )
    return copies


def shifted(unit, by):
    return lambda half: unit(half + by)


def link_0_kernel(b_ref, four, third, part_ref, y_ref, inverse, held, sems):
    unit = first_chunk_unit(four, third)
    first = fetch_inverse(unit, inverse, sems.at[0])
    second = fetch_block(shifted(unit, 2), held, 0, sems.at[1])
    wait_all(first)
    solved = solve(inverse, b_ref[...])
    y_ref[...] = solved
    part_ref[...] = update(held, [solved], [functools.partial(wait_all, second)])


def link_1_kernel(b_ref, own, got, y0_ref, four, third, n0, n1, f0, f1, *refs):
    part_ref, y_ref, inverse, held, sems = refs
    first = fetch_inverse(shifted(first_chunk_unit(four, third), 4), inverse, sems.at[0])
    unit = block_unit((n0, n1), (f0, f1))
    copies = [fetch_block(shifted(unit, 2 * t), held, t, sems.at[t + 1]) for t in range(2)]
    wait_all(first)
    solved = solve(inverse, b_ref[...] - (own[...] + got[...]))
    y_ref[...] = solved
    waits = [functools.partial(wait_all, c) for c in copies]
    part_ref[...] = update(held, [y0_ref[...], solved], waits)


def link_2_kernel(b_ref, s0, s1, s2, s3, y0_ref, y1_ref, n0, n1, f0, f1, root, swapped, *refs):
    part_ref, y_ref, inverse, held, sems = refs
    unit = block_unit((n0, n1), (f0, f1))
    root, swapped = root_unit(root), root_unit(swapped)
    first = fetch_inverse(root, inverse, sems.at[0], swapped, 0)
    copies = [fetch_block(shifted(unit, 2 * t + 4), held, t, sems.at[t + 1]) for t in range(2)]
    copies.append(fetch_halves(root, swapped, held, 2, sems.at[3]))
    wait_all(first)
    solved = solve(inverse, b_ref[...] - sum_four((s0, s1, s2, s3)))
    y_ref[...] = solved
    waits = [functools.partial(wait_all, c) for c in copies]
    last = jnp.where(spot()[4] == 0, solved, 0.0)
    part_ref[...] = update(held, [y0_ref[...], y1_ref[...], last], waits)


def link_3_kernel(b_ref, s0, s1, s2, s3, y0_ref, y1_ref, y2_ref, root, swapped, *refs):
    outs, (pieces, inverse, sems) = refs[:4], refs[4:]
    first = fetch_inverse(root_unit(root), inverse, sems.at[0], root_unit(swapped), 1)
    vector = b_ref[...] - sum_four((s0, s1, s2, s3))
    lay_values((y0_ref, y1_ref, y2_ref), pieces)
    wait_all(first)
    pieces[:, 3] = solve(inverse, vector).T.reshape(4, 32, 128)
    _, zh, _, x, _ = spot()
    for b1 in range(2):
        for b2 in range(2):
            outs[b1 * 2 + b2][...] = pieces[(zh ^ b1) * 2 + (x ^ b2)]


def link_scratch(nblocks, nsems):
    blocks = [pltpu.VMEM((nblocks, 2, 2, 2, 2, 2, 32, 128), F32)] if nblocks else []
    return (
        [pltpu.VMEM((2, 2, 2, 2, 2, 32, 128), F32)] + blocks + [pltpu.SemaphoreType.DMA((nsems, 2, 8))]
    )


def root_kernel(four, third, n0, n1, f0, f1, out):
    for b1 in range(2):
        for b3 in range(2):
            for b2 in range(2):
                place = b1 * 4 + b3 * 2 + b2
                for unit in range(2):
                    out[place, unit] = (four, third)[b3][b2 * 2 + b1, 6 + unit]
                out[place, 2] = ((n0, n1), (f0, f1))[b1][b3][b2, 8]


def lay_values(refs, held):
    for p, ref in enumerate(refs):
        held[:, p] = ref[...].T.reshape(4, 32, 128)


def stand_kernel(near_ref, other_ref, *refs):
    outs, held = refs[:4], refs[4]
    _, zh, zl, x, _ = spot()
    for b1 in range(2):
        for b2 in range(2):
            for b, source in enumerate((near_ref, other_ref)):
                held[((zh ^ b1) * 2 + (zl ^ b)) * 2 + (x ^ b2)] = source[b1 * 2 + b2]
    for p, out in enumerate(outs):
        out[...] = held[:, p].reshape(256, 128).T


def join_kernel(near_ref, other_ref, out_ref, held):
    r, zh, _, x, core = spot()
    near = r ^ core
    for b1 in range(2):
        for b2 in range(2):
            place = (zh ^ b1) * 2 + (x ^ b2)
            held[near * 4 + place] = near_ref[b1 * 2 + b2]
            held[(near ^ 1) * 4 + place] = other_ref[b1 * 2 + b2]
    for p in range(2):
        for u in range(4):
            lanes = slice(u * 128, u * 128 + 128)
            out_ref[p, 0, :, lanes], out_ref[p, 1, :, lanes] = swap_lanes(
                held[2 * u, p], held[2 * u + 1, p]
            )


def join(name, near, other):
    return pl.pallas_call(
        join_kernel,
        out_shape=shaped(2, 2, 32, 512),
        in_specs=[vmem()] * 2,
        out_specs=vmem(),
        scratch_shapes=[pltpu.VMEM((8, 2, 32, 128), F32)],
        compiler_params=pltpu.CompilerParams(vmem_limit_bytes=VMEM_OF_A_KERNEL),

        name=name,
    )(*(pltpu.with_memory_space_constraint(v, pltpu.VMEM) for v in (near, other)))


def to_groups(parts):
    return [parts[0]] + [send(parts[k], to_group(k // 2, k % 2)) for k in (1, 2, 3)]


VECTOR = [(128, 256), (128, 128)]


def grouped(leaf_rhs, root_rhs, leaf_inverses, root_inverses, leaf_blocks, root_block, pattern):
    zl = (lax.axis_index("col") // 2) % 2

    def whole(keep, got):
        return jnp.stack([jnp.where(zl == 0, keep, got), jnp.where(zl == 0, got, keep)])

    def first_chunk(values, got):
        return jnp.concatenate(
            [whole(values[0], got[0]), values[1:3], whole(values[3], got[1]), whole(values[4], got[2])]
        )

    away, first, blocks, *cuts = begin(
        pattern, leaf_inverses, leaf_blocks, leaf_rhs, root_rhs, root_inverses, root_block
    )
    first_far = send(first, to_far)
    first_far_pair = send(away, to_far_pair)
    pair = send(away, to_pair)
    second_own = send(blocks, to_second)
    moved = to_groups(cuts)

    near_0 = jnp.stack([blocks, second_own])
    near_1 = send(near_0, to_third)
    first_far = after(first_far, near_0)
    two_a = jnp.stack([first_chunk(first, pair), first_chunk(first_far, first_far_pair)])
    second_a = send(two_a, to_second)
    far = send(after(blocks, two_a), to_far)
    rhs_in = jnp.stack(after(moved, two_a))
    rhs_pair = send(rhs_in, to_pair)

    four_a = jnp.concatenate([two_a, after(second_a, near_1, rhs_in)])
    third_a = send(four_a, to_third)
    b0, b1, r2, r3 = call(
        "stand",
        stand_kernel,
        [(128, 256)] * 4,
        after(rhs_in, four_a),
        rhs_pair,
        scratch=[pltpu.VMEM((8, 4, 32, 128), F32)],
    )
    far = after(far, b0)
    far_0 = jnp.stack([far, send(far, to_second)])
    far_1 = send(far_0, to_third)

    own, y0 = call(
        "link_0",
        link_0_kernel,
        VECTOR,
        after(b0, far_0),
        four_a,
        third_a,
        scratch=link_scratch(1, 2),
    )
    got = send(own, to_pair)

    own, y1 = call(
        "link_1",
        link_1_kernel,
        VECTOR,
        b1,
        own,
        got,
        y0,
        four_a,
        third_a,
        near_0,
        near_1,
        far_0,
        far_1,
        scratch=link_scratch(2, 3),
    )
    sums = [own, send(own, to_core), send(own, to_pair), send(own, to_pair_core)]
    (root_own,) = call(
        "root_shards",
        root_kernel,
        [(8, 3, 2, 32, 128)],
        after(four_a, own),
        third_a,
        near_0,
        near_1,
        far_0,
        far_1,
    )
    root_swapped = send(root_own, to_core)

    own, y2 = call(
        "link_2",
        link_2_kernel,
        VECTOR,
        r2,
        *sums,
        y0,
        y1,
        near_0,
        near_1,
        far_0,
        far_1,
        root_own,
        root_swapped,
        scratch=link_scratch(3, 4),
    )
    sums = [own, send(own, to_core), send(own, to_pair), send(own, to_pair_core)]
    parts = call(
        "link_3",
        link_3_kernel,
        [(4, 32, 128)] * 4,
        r3,
        *sums,
        y0,
        y1,
        y2,
        root_own,
        root_swapped,
        scratch=[pltpu.VMEM((4, 4, 32, 128), F32)] + link_scratch(0, 1),
    )
    moved = jnp.stack([send(parts[k], to_group_by_core(k // 2, k % 2)) for k in range(4)])
    leaf_near, root_near = moved[:, :2], moved[:, 2:]
    leaf_other = send(leaf_near, to_row)
    root_other = send(root_near, to_core)
    return (
        join("join_leaf", leaf_near, leaf_other)[None],
        join("join_root", root_near, root_other),
    )


def solution(mesh):
    placed = (
        P("leaf", None, None, "col", None),
        P(None, None, "col", None),
        P("leaf", None, None, "col", "row"),
        P(None, None, "col", "row"),
        P("leaf", None, None, "col", "row"),
        P(None, "col", "row"),
        P("leaf", None, "row", "col"),
    )
    small = (mesh.shape["row"], mesh.shape["col"], mesh.shape["leaf"]) == (2, 8, 2)
    return jax.shard_map(
        grouped if small else general,
        mesh=mesh,
        in_specs=placed,
        out_specs=(P("leaf", None, None, "col", None), P(None, None, "col", None)),
        check_vma=False,
    )
```
